512 devices in a mesh: gx: 128 (over y_hi, x, z), gy: 4 (over y_lo, core).
Axes of the slice: x: 4, y: 4 (y_hi: 2, y_lo: 2; y = y_hi * 2 + y_lo), z: 16, core: 2. Of those that a mesh axis runs over, the one named last changes fastest.
Arguments:
- trans: float32 [13, 256, 4096], P(None, 'gx', 'gy'), may hold values from 0.1 to 1
- storage: float32 [256, 4096], P('gx', 'gy'), may hold values from 0.05 to 1
- fault_cells: int32 [128, 4, 512], P('gx', 'gy'), may hold values from 0 to 2047, as said below
- fault_count: int32 [128, 4], P('gx', 'gy'), may hold values from 0 to 512, as said below
- fault_trans: float32 [128, 4, 512], P('gx', 'gy'), may hold values from 0.1 to 1, as said below
Outputs:
- coarse_columns: float32 [125, 128, 1024], P(None, 'gx', 'gy')
The draws below stay inside these ranges and needn't reach their ends.
Inputs may be any that keep to these rules, and one draw needn't show every extreme that they name: `fault_cells`: on a device with even gx index every slot's cell lies at x' = 1, on one with odd gx index at x' = 0; slot k of the partners with gx indices 2j and 2j + 1 (same gy index) has equal y' and layers z differing by at most 8. `fault_count`: equal on devices whose gx indices are 2j and 2j + 1 with the same gy index; some device has 512. `fault_trans`: equal slot by slot on devices whose gx indices are 2j and 2j + 1 with the same gy index.
All inputs are finite; a program needn't handle non-finite values.
Results may differ from the reference program's by a relative error of at most 0.0003.
Values sent between devices are 32-bit elements; how exact they have to be, the bound alone decides.
A program may use at most 64 MiB of HBM per device.

```python
import math
import jax
import jax.numpy as jnp
from jax import lax

CX = 2
CY = 8
NZ = 128
FMAX = 512
COLORS = 125
NX = 256
NY = 32
GX_HALF = 64
GY_COUNT = 4
N_GX = 128
N_GY = 4


def draw_fault_cells(key, part):
    base = jax.random.fold_in(key, 5)
    shape = (GX_HALF, GY_COUNT, FMAX)
    column = jax.random.randint(jax.random.fold_in(base, 1), shape, 0, CY)
    depth = jax.random.randint(jax.random.fold_in(base, 2), shape, 0, NZ)
    throw = jax.random.randint(jax.random.fold_in(base, 3), shape, -8, 9)
    facing = jnp.clip(depth + throw, 0, NZ - 1)
    lower = ((CX - 1) * CY + column) * NZ + depth
    upper = column * NZ + facing
    joined = jnp.stack([lower, upper], axis=1)
    return joined.reshape(2 * GX_HALF, GY_COUNT, FMAX).astype(jnp.int32)


def draw_fault_count(key, part):
    level = jax.random.randint(key, (GX_HALF, GY_COUNT), 0, 8)
    base = FMAX * (1 + level * level) // 50
    base = base.at[0, 0].set(FMAX)
    return jnp.repeat(base, 2, axis=0).astype(jnp.int32)


def draw_fault_trans(key, part):
    spread = jax.random.uniform(jax.random.fold_in(key, 17), (GX_HALF, GY_COUNT, FMAX), jnp.float32)
    base = jnp.exp(jnp.log(0.1) + jnp.log(10.0) * spread)
    base = jnp.clip(base, 0.1, 1.0)
    return jnp.repeat(base, 2, axis=0).astype(jnp.float32)


def level_of(rng, dims, cuts, smallest, top_value):
    def one(position, shards_of):
        heights = jax.random.uniform(jax.random.fold_in(jax.random.fold_in(rng, 6), position), (shards_of,), jnp.float32, smallest / len(cuts), top_value / len(cuts))
        return jnp.repeat(jnp.exp(heights), dims[position] // shards_of).reshape((-1,) + (1,) * (len(dims) - position - 1))

    loudness = one(*cuts[0])
    for cut in cuts[1:]:
        loudness = loudness * one(*cut)
    return loudness


def setup_inputs(seed: int = 0) -> dict:
    arg_keys = jax.random.split(jax.random.key(seed), 6)
    return {
        "trans": jnp.clip(jnp.exp(math.log(1.0) - 2.3025851 * jax.random.uniform(arg_keys[0], (13, NX, NY * NZ), jnp.float32) ** level_of(arg_keys[0], (13, NX, NY * NZ), ((1, 128), (2, 4)), -0.2, 0.2)), 0.1, 1.0),
        "storage": jnp.clip(jnp.exp(math.log(1.0) - 2.9957323 * jax.random.uniform(arg_keys[1], (NX, NY * NZ), jnp.float32) ** level_of(arg_keys[1], (NX, NY * NZ), ((0, 128), (1, 4)), -0.2, 0.2)), 0.05, 1.0),
        "fault_cells": draw_fault_cells(jax.random.fold_in(arg_keys[5], 71), 0),
        "fault_count": draw_fault_count(jax.random.fold_in(arg_keys[5], 71), 0),
        "fault_trans": draw_fault_trans(jax.random.fold_in(arg_keys[5], 71), 0),
    }


FORWARD = ((0, 0, 1), (0, 1, -1), (0, 1, 0), (0, 1, 1), (1, -1, -1), (1, -1, 0), (1, -1, 1), (1, 0, -1), (1, 0, 0), (1, 0, 1), (1, 1, -1), (1, 1, 0), (1, 1, 1))
damping = 2.0 / 3.0
tentative_value = 0.35355339059327373


def shifted(padded, step_x, step_y, step_z, size_x, size_y, size_z):
    return padded[..., 1 + step_x:1 + step_x + size_x, 1 + step_y:1 + step_y + size_y, 1 + step_z:1 + step_z + size_z]


def global_index(local_cells, grid_y, layers):
    device_x = jnp.arange(N_GX, dtype=jnp.int32)[:, None, None]
    device_y = jnp.arange(N_GY, dtype=jnp.int32)[None, :, None]
    place_x = device_x * CX + local_cells // (CY * NZ)
    place_y = device_y * CY + (local_cells // NZ) % CY
    place_z = local_cells % NZ
    return ((place_x * grid_y + place_y) * layers + place_z).astype(jnp.int32)


def reference(trans, storage, fault_cells, fault_count, fault_trans):
    layers = NZ
    grid_x = storage.shape[0]
    grid_y = storage.shape[1] // layers
    cell_count = grid_x * grid_y * layers
    coord_x = jnp.arange(grid_x, dtype=jnp.int32)[:, None, None]
    coord_y = jnp.arange(grid_y, dtype=jnp.int32)[None, :, None]
    coord_z = jnp.arange(layers, dtype=jnp.int32)[None, None, :]
    weights = trans.reshape(13, grid_x, grid_y, layers)
    pieces = []
    for offset, step in enumerate(FORWARD):
        inside = (coord_x + step[0] >= 0) & (coord_x + step[0] < grid_x) & (coord_y + step[1] >= 0) & (coord_y + step[1] < grid_y) & (coord_z + step[2] >= 0) & (coord_z + step[2] < layers)
        pieces.append(jnp.where(inside, weights[offset], jnp.float32(0.0)))
    masked = jnp.stack(pieces)
    widened = jnp.pad(masked, ((0, 0), (1, 1), (1, 1), (1, 1)))
    behind_sum = jnp.zeros((grid_x, grid_y, layers), jnp.float32)
    for offset, step in enumerate(FORWARD):
        behind_sum = behind_sum + shifted(widened[offset], -step[0], -step[1], -step[2], grid_x, grid_y, layers)
    slots = jnp.arange(FMAX, dtype=jnp.int32)[None, None, :]
    live_trans = jnp.where(slots < fault_count[:, :, None], fault_trans, jnp.float32(0.0))
    own_grid = global_index(fault_cells, grid_y, layers)
    own_index = own_grid.reshape(-1)
    partner_index = jnp.flip(own_grid.reshape(GX_HALF, 2, N_GY, FMAX), axis=1).reshape(-1).astype(jnp.int32)
    live_flat = live_trans.reshape(-1)
    fault_diag = jnp.zeros((cell_count,), jnp.float32).at[own_index].add(live_flat).reshape(grid_x, grid_y, layers)
    diagonal = storage.reshape(grid_x, grid_y, layers) + jnp.sum(masked, 0) + behind_sum + fault_diag

    def apply_operator(field):
        padded = jnp.pad(field, 1)
        summed = diagonal * field
        for offset, step in enumerate(FORWARD):
            summed = summed - masked[offset] * shifted(padded, step[0], step[1], step[2], grid_x, grid_y, layers) - shifted(widened[offset], -step[0], -step[1], -step[2], grid_x, grid_y, layers) * shifted(padded, -step[0], -step[1], -step[2], grid_x, grid_y, layers)
        across = jnp.zeros((cell_count,), jnp.float32).at[own_index].add(live_flat * field.reshape(-1)[partner_index])
        return summed - across.reshape(grid_x, grid_y, layers)

    def one_colour(colour):
        agrees = ((coord_x // 2) % 5 == colour // 25) & ((coord_y // 2) % 5 == (colour // 5) % 5) & ((coord_z // 2) % 5 == colour % 5)
        probes = jnp.where(agrees, jnp.float32(tentative_value), jnp.float32(0.0))
        first = apply_operator(probes)
        smoothed = probes - damping * first / diagonal
        applied = apply_operator(smoothed)
        scaled = applied / diagonal
        result = applied - damping * apply_operator(scaled)
        coarse = result.reshape(grid_x // 2, 2, grid_y // 2, 2, layers // 2, 2).sum((1, 3, 5))
        return (tentative_value * coarse).reshape(grid_x // 2, (grid_y // 2) * (layers // 2))

    return lax.map(one_colour, jnp.arange(COLORS, dtype=jnp.int32))
```

```python
import jax
import jax.numpy as jnp
from jax import lax
from jax.experimental import pallas as pl
from jax.experimental.pallas import tpu as pltpu
from jax.sharding import PartitionSpec as P

FORWARD = (
    (0, 0, 1),
    (0, 1, -1),
    (0, 1, 0),
    (0, 1, 1),
    (1, -1, -1),
    (1, -1, 0),
    (1, -1, 1),
    (1, 0, -1),
    (1, 0, 0),
    (1, 0, 1),
    (1, 1, -1),
    (1, 1, 0),
    (1, 1, 1),
)
damping = 2.0 / 3.0
tent = 0.35355339059327373
F32 = jnp.float32


def kid(dx, dy, dz):
    return (dx + 1) * 9 + (dy + 1) * 3 + dz + 1


def body(meta, c_ref, f_ref, out_ref, kf, inv_ref, fd, pat, bands, fp, gs, s3, ap, b3, acc_ref):
    gx = meta[0]
    gy = meta[1]
    odd_dev = lax.rem(gx, 2)
    zl = lax.broadcasted_iota(jnp.int32, (16, 128), 1)
    yi = lax.broadcasted_iota(jnp.int32, (16, 128), 0)
    yg = gy * 8 + yi - 3
    y_odd = lax.rem(yi, 2) == 0

    e8 = lax.broadcasted_iota(jnp.int32, (8, 128), 0)
    z8 = lax.broadcasted_iota(jnp.int32, (8, 128), 1)
    for d in range(17):
        col = lax.rem(lax.shift_right_logical(z8 + (d - 8 + 160), 1), 5)
        pat[d] = jnp.where(col == e8, F32(1.0), F32(0.0))

    wsum = [jnp.zeros((16, 128), F32) for _ in range(6)]
    for o, (dx, dy, dz) in enumerate(FORWARD):
        ok = (yg + dy >= 0) & (yg + dy < 32) & (zl + dz >= 0) & (zl + dz < 128)
        for x in range(-3, 4):
            if dx == 0 and x == -3:
                continue
            m = jnp.where(ok, c_ref[o, x + 3], F32(0.0))
            if dx:
                m = m * (2 * gx + x + 1 < 256).astype(F32)
            if x >= -2:
                kf[kid(dx, dy, dz), x + 2] = -m
                wsum[x + 2] = wsum[x + 2] + m
            xb = x + dx
            if -2 <= xb <= 3:
                b = m
                if dy:
                    b = pltpu.roll(b, dy % 16, 0)
                if dz:
                    b = pltpu.roll(b, dz % 128, 1)
                kf[kid(-dx, -dy, -dz), xb + 2] = -b
                wsum[xb + 2] = wsum[xb + 2] + b

    x_own = 1 - odd_dev
    x_par = 2 - 3 * odd_dev
    x_oth = 5 * odd_dev - 2
    sides = ((0, 1, 2), (1, 0, 2), (3, 4, 5))
    d24 = lax.broadcasted_iota(jnp.int32, (24, 512), 0) - 8
    for dev, (ylo, ny, yout) in enumerate(((6, 2, 0), (0, 8, 2), (0, 2, 10))):
        for side, (own, par, tr) in enumerate(sides):
            co = f_ref[dev, own : own + 1].astype(jnp.int32) & 1023
            cp = f_ref[dev, par : par + 1].astype(jnp.int32) & 1023
            t = f_ref[dev, tr : tr + 1]
            delta = (cp & 127) - (co & 127)
            bt = jnp.where(d24 == delta, t, F32(0.0))
            hi = bt.astype(jnp.bfloat16)
            r1 = bt - hi.astype(F32)
            mid = r1.astype(jnp.bfloat16)
            low = (r1 - mid.astype(F32)).astype(jnp.bfloat16)
            rows = lax.broadcasted_iota(jnp.int32, (ny * 128, 512), 0) + ylo * 128
            hot = jnp.where(rows == co, F32(1.0), F32(0.0)).astype(jnp.bfloat16)
            dims = (((1,), (1,)), ((), ()))
            got = lax.dot_general(hi, hot, dims, preferred_element_type=F32)
            got = got + lax.dot_general(mid, hot, dims, preferred_element_type=F32)
            got = got + lax.dot_general(low, hot, dims, preferred_element_type=F32)
            for y in range(ny):
                bands[side, yout + y] = got[:, y * 128 : (y + 1) * 128]

    fd[...] = jnp.zeros((6, 16, 128), F32)
    for side, xs in enumerate((x_own, x_par, x_oth)):
        for y in range(12):
            tile = jnp.zeros((8, 128), F32)
            for d in range(17):
                tile = tile + bands[side, y, d : d + 1, :] * pat[d]
            fp[side, y] = tile
            fd[xs + 2, y + 1 : y + 2, :] = jnp.sum(tile, axis=0, keepdims=True)

    for x in range(-2, 4):
        diag = c_ref[13, x + 3] + wsum[x + 2] + fd[x + 2]
        inv = jnp.where(diag > 0.0, 1.0 / diag, F32(0.0))
        kf[13, x + 2] = diag
        inv_ref[x + 2] = inv
        for dz in (-1, 0, 1):
            low, high = [], []
            for dx in (-1, 0, 1):
                mid = kf[kid(dx, 0, dz), x + 2]
                low.append(kf[kid(dx, -1, dz), x + 2] + jnp.where(y_odd, mid, F32(0.0)))
                high.append(kf[kid(dx, 1, dz), x + 2] + jnp.where(y_odd, F32(0.0), mid))
            for ry, part in enumerate((low, high)):
                if x % 2:
                    pair = (part[0] + part[1], part[2])
                else:
                    pair = (part[0], part[1] + part[2])
                for rx, total in enumerate(pair):
                    g = inv * total * F32(-damping * tent)
                    if dz == 0 and rx == (0 if x % 2 else 1):
                        mine = y_odd if ry == 0 else jnp.logical_not(y_odd)
                        g = g + jnp.where(mine, F32(tent), F32(0.0))
                    gs[x + 2, rx * 2 + ry, dz + 1] = g

    def smooth(y, carry):
        for x in range(6):
            for r in range(4):
                tile = gs[x, r, 0, pl.ds(y + 1, 1), :] * pat[7]
                tile = tile + gs[x, r, 1, pl.ds(y + 1, 1), :] * pat[8]
                tile = tile + gs[x, r, 2, pl.ds(y + 1, 1), :] * pat[9]
                s3[1, x, y, r] = tile
        ry = 1 - lax.rem(y, 2)
        for side, xs in enumerate((x_own, x_par, x_oth)):
            rx = xs & 1
            iv = inv_ref[xs + 2, pl.ds(y + 1, 1), :] * F32(damping * tent)
            s3[1, xs + 2, y, rx * 2 + ry] += iv * fp[side, y]
        for x in range(6):
            for r in range(4):
                tile = s3[1, x, y, r]
                s3[0, x, y, r] = pltpu.roll(tile, 1, 1)
                s3[2, x, y, r] = pltpu.roll(tile, 127, 1)
        return carry

    lax.fori_loop(0, 12, smooth, 0)

    def apply_pair(t, carry):
        for x in range(-1, 3):
            for p in range(2):
                y = p - 1
                acc = [None] * 9
                for dx in (-1, 0, 1):
                    for dy in (-1, 0, 1):
                        xn, yn = x + dx, y + dy
                        bx = (xn - 1) // 2 - (x // 2 - 1)
                        by = (yn - 1) // 2 - (y // 2 - 1)
                        for dz in (-1, 0, 1):
                            row = kf[kid(dx, dy, dz), x + 2, pl.ds(2 * t + y + 3, 1), :]
                            for rx in range(2):
                                for ry in range(2):
                                    q = (bx + rx) * 3 + by + ry
                                    v = row * s3[dz + 1, xn + 2, 2 * t + yn + 2, rx * 2 + ry]
                                    acc[q] = v if acc[q] is None else acc[q] + v
                for q in range(9):
                    ap[x + 1, 2 * t + y + 1, q] = acc[q]
        return carry

    lax.fori_loop(0, 5, apply_pair, 0)

    def apply_fault(n, carry):
        y = n - 1
        y_is_odd = y & 1
        for side, (xs, xn) in enumerate(((x_own, x_par), (x_par, x_own))):
            for rx in range(2):
                for ry in range(2):
                    tile = s3[1, xn + 2, n + 1, rx * 2 + ry]
                    total = jnp.zeros((8, 128), F32)
                    for d in range(17):
                        row = bands[side, n + 1, d : d + 1, :]
                        total = total + row * pltpu.roll(tile, (8 - d) % 128, 1)
                    q = ((xs & 1) + rx) * 3 + y_is_odd + ry
                    ap[xs + 1, n, q] -= total
        for x in range(4):
            iv = inv_ref[x + 1, pl.ds(n + 2, 1), :]
            for q in range(9):
                tile = ap[x, n, q] * iv
                b3[1, x, n, q] = tile
                b3[0, x, n, q] = pltpu.roll(tile, 1, 1)
                b3[2, x, n, q] = pltpu.roll(tile, 127, 1)
        return carry

    lax.fori_loop(0, 10, apply_fault, 0)

    pz = lax.broadcasted_iota(jnp.int32, (128, 64), 0)
    pc = lax.broadcasted_iota(jnp.int32, (128, 64), 1)
    pick = jnp.where(lax.shift_right_logical(pz, 1) == pc, F32(tent), F32(0.0))

    def restrict(yc, carry):
        acc = [None] * 25
        for xn in range(-1, 3):
            for yn in range(-1, 3):
                bx, by = xn // 2 + 1, yn // 2 + 1
                for dz in (-1, 0, 1):
                    row = None
                    for x in (0, 1):
                        for y in (0, 1):
                            if abs(xn - x) <= 1 and abs(yn - y) <= 1:
                                k = kf[kid(xn - x, yn - y, dz), x + 2, pl.ds(2 * yc + y + 3, 1), :]
                                row = k if row is None else row + k
                    row = row * F32(-damping)
                    if dz == 0 and xn in (0, 1) and yn in (0, 1):
                        row = row + kf[13, xn + 2, pl.ds(2 * yc + yn + 3, 1), :]
                    for rx in range(3):
                        for ry in range(3):
                            q = (bx + rx) * 5 + by + ry
                            v = row * b3[dz + 1, xn + 1, 2 * yc + yn + 1, rx * 3 + ry]
                            acc[q] = v if acc[q] is None else acc[q] + v
        for q in range(25):
            acc_ref[q // 5, q % 5] = acc[q]
        far = lax.shift_right_arithmetic(x_par, 1) + 1
        for rx in range(3):
            for ry in range(3):
                total = jnp.zeros((8, 128), F32)
                for y in range(2):
                    tile = b3[1, x_par + 1, 2 * yc + y + 1, rx * 3 + ry]
                    for d in range(17):
                        row = bands[0, 2 * yc + y + 2, d : d + 1, :]
                        total = total + row * pltpu.roll(tile, (8 - d) % 128, 1)
                acc_ref[far + rx, 1 + ry] += total * F32(damping)
        got = jnp.dot(
            acc_ref[...].reshape(200, 128),
            pick,
            precision=lax.Precision.HIGHEST,
            preferred_element_type=F32,
        )
        for rx in range(5):
            a = lax.rem(gx + rx + 3, 5)
            for ry in range(5):
                b = lax.rem(gy * 4 + yc + ry + 3, 5)
                q = (rx * 5 + ry) * 8
                out_ref[a, b, yc] = got[q : q + 8]
        return carry

    lax.fori_loop(0, 4, restrict, 0)


def per_device(trans, storage, fault_cells, fault_count, fault_trans):
    gx = lax.axis_index("gx")
    gy = lax.axis_index("gy")
    n_gx = lax.axis_size("gx")
    n_gy = lax.axis_size("gy")
    slots = jnp.arange(512, dtype=jnp.int32)
    live = jnp.where(slots < fault_count.reshape(()), fault_trans.reshape(-1), F32(0.0))
    cells = fault_cells.reshape(-1).astype(F32)
    fault = jnp.concatenate([cells.reshape(4, 128), live.reshape(4, 128)], axis=0)
    core = jnp.concatenate(
        [trans.reshape(13, 2, 8, 128), storage.reshape(1, 2, 8, 128)], axis=0
    )

    def shift(value, axis, size, by):
        pairs = [(i, i + by) for i in range(size) if 0 <= i + by < size]
        return lax.ppermute(value, axis, pairs)

    packed = jnp.concatenate([core.reshape(224, 128), fault], axis=0)
    left = shift(packed, "gx", n_gx, 1)
    right = shift(packed, "gx", n_gx, -1)
    second = jnp.concatenate([core[4:13, 1].reshape(72, 128), fault], axis=0)
    left2 = shift(second, "gx", n_gx, 2)
    right2 = shift(fault, "gx", n_gx, -2)
    far = jnp.concatenate(
        [
            jnp.zeros((4, 1, 8, 128), F32),
            left2[:72].reshape(9, 1, 8, 128),
            jnp.zeros((1, 1, 8, 128), F32),
        ],
        axis=0,
    )
    wide = jnp.concatenate(
        [far, left[:224].reshape(14, 2, 8, 128), core, right[:224].reshape(14, 2, 8, 128)], axis=1
    )
    even = lax.rem(gx, 2) == 0
    partner = jnp.where(even, right[224:228], left[224:228])
    other = jnp.where(even, left[224:], right[224:])
    beyond = jnp.where(even, left2[72:76], right2[:4])
    faults = jnp.concatenate([fault[:4], partner, fault[4:], other[:4], beyond, other[4:]], axis=0)
    up = jnp.concatenate([wide[:, :, 5:].reshape(294, 128), faults], axis=0)
    down = jnp.concatenate([wide[:, :, :3].reshape(294, 128), faults], axis=0)
    below = shift(up, "gy", n_gy, 1)
    above = shift(down, "gy", n_gy, -1)
    full = jnp.concatenate(
        [
            below[:294].reshape(14, 7, 3, 128),
            wide,
            above[:294].reshape(14, 7, 3, 128),
            jnp.zeros((14, 7, 2, 128), F32),
        ],
        axis=2,
    )
    slots3 = jnp.stack([below[294:], faults, above[294:]]).reshape(3, 6, 512)
    meta = jnp.stack([gx, gy]).astype(jnp.int32)
    vm = pl.BlockSpec(memory_space=pltpu.VMEM)
    out = pl.pallas_call(
        body,
        out_shape=jax.ShapeDtypeStruct((5, 5, 4, 8, 64), F32),
        in_specs=[pl.BlockSpec(memory_space=pltpu.SMEM), vm, vm],
        out_specs=vm,
        scratch_shapes=[
            pltpu.VMEM((27, 6, 16, 128), F32),
            pltpu.VMEM((6, 16, 128), F32),
            pltpu.VMEM((6, 16, 128), F32),
            pltpu.VMEM((17, 8, 128), F32),
            pltpu.VMEM((3, 12, 24, 128), F32),
            pltpu.VMEM((3, 12, 8, 128), F32),
            pltpu.VMEM((6, 4, 3, 16, 128), F32),
            pltpu.VMEM((3, 6, 12, 4, 8, 128), F32),
            pltpu.VMEM((4, 10, 9, 8, 128), F32),
            pltpu.VMEM((3, 4, 10, 9, 8, 128), F32),
            pltpu.VMEM((5, 5, 8, 128), F32),
        ],
        compiler_params=pltpu.CompilerParams(vmem_limit_bytes=48 * 1024 * 1024),
    )(meta, full, slots3)
    return out[:, :, :, :5].transpose(0, 1, 3, 2, 4).reshape(125, 1, 256)


def solution(mesh):
    placed = (
        P(None, "gx", "gy"),
        P("gx", "gy"),
        P("gx", "gy", None),
        P("gx", "gy"),
        P("gx", "gy", None),
    )
    return jax.shard_map(
        per_device, mesh=mesh, in_specs=placed, out_specs=P(None, "gx", "gy"), check_vma=False
    )
```

```python
import jax
import jax.numpy as jnp
from jax import lax
from jax.experimental import pallas as pl
from jax.experimental.pallas import tpu as pltpu
from jax.sharding import PartitionSpec as P

FORWARD = (
    (0, 0, 1),
    (0, 1, -1),
    (0, 1, 0),
    (0, 1, 1),
    (1, -1, -1),
    (1, -1, 0),
    (1, -1, 1),
    (1, 0, -1),
    (1, 0, 0),
    (1, 0, 1),
    (1, 1, -1),
    (1, 1, 0),
    (1, 1, 1),
)
damping = 2.0 / 3.0
tent = 0.35355339059327373
F32 = jnp.float32


def kid(dx, dy, dz):
    return (dx + 1) * 9 + (dy + 1) * 3 + dz + 1


def body(c_ref, f_ref, out_ref, kf, inv_ref, fd, pat, bands, fp, gs, s3, ap, b3, acc_ref):
    gx = lax.axis_index("gx")
    gy = lax.axis_index("gy")
    odd_dev = lax.rem(gx, 2)
    zl = lax.broadcasted_iota(jnp.int32, (16, 128), 1)
    yi = lax.broadcasted_iota(jnp.int32, (16, 128), 0)
    yg = gy * 8 + yi - 3
    y_in = (yg >= 0) & (yg < 32)
    y_odd = lax.rem(yi, 2) == 0

    e8 = lax.broadcasted_iota(jnp.int32, (8, 128), 0)
    z8 = lax.broadcasted_iota(jnp.int32, (8, 128), 1)
    for d in range(17):
        col = lax.rem(lax.shift_right_logical(z8 + (d - 8 + 160), 1), 5)
        pat[d] = jnp.where(col == e8, F32(1.0), F32(0.0))

    wsum = [jnp.zeros((16, 128), F32) for _ in range(6)]
    for o, (dx, dy, dz) in enumerate(FORWARD):
        ok = y_in & (yg + dy >= 0) & (yg + dy < 32) & (zl + dz >= 0) & (zl + dz < 128)
        for x in range(-3, 4):
            if dx == 0 and x == -3:
                continue
            xg = jnp.full((16, 128), 2 * gx + x, jnp.int32)
            x_ok = (xg >= 0) & (xg + dx < 256)
            m = jnp.where(ok & x_ok, c_ref[o, x + 3], F32(0.0))
            if x >= -2:
                kf[kid(dx, dy, dz), x + 2] = -m
                wsum[x + 2] = wsum[x + 2] + m
            xb = x + dx
            if -2 <= xb <= 3:
                b = m
                if dy:
                    b = pltpu.roll(b, dy % 16, 0)
                if dz:
                    b = pltpu.roll(b, dz % 128, 1)
                kf[kid(-dx, -dy, -dz), xb + 2] = -b
                wsum[xb + 2] = wsum[xb + 2] + b

    x_own = 1 - odd_dev
    x_par = 2 - 3 * odd_dev
    x_oth = 5 * odd_dev - 2
    s_par = 3 - 2 * odd_dev
    s_oth = 1 + 2 * odd_dev
    s_far = 4 * odd_dev
    sides = ((2, s_par, 2), (s_par, 2, 2), (s_oth, s_far, s_oth))

    def slot_row(dev, place, first):
        rows = [f_ref[dev, place, first + i : first + i + 1, :] for i in range(4)]
        return jnp.concatenate(rows, axis=1)

    d24 = lax.broadcasted_iota(jnp.int32, (24, 512), 0) - 8
    for dev, (ylo, ny, yout) in enumerate(((6, 2, 0), (0, 8, 2), (0, 2, 10))):
        for side, (own, par, tr) in enumerate(sides):
            co = slot_row(dev, own, 0).astype(jnp.int32) & 1023
            cp = slot_row(dev, par, 0).astype(jnp.int32) & 1023
            reach = (gy + dev >= 1) & (gy + dev < 5)
            if side == 2:
                mate = gx + 4 * odd_dev - 2
                reach = reach & (mate >= 0) & (mate < 128)
            known = jnp.full((1, 512), reach.astype(jnp.int32), jnp.int32) > 0
            t = jnp.where(known, slot_row(dev, tr, 4), F32(0.0))
            delta = (cp & 127) - (co & 127)
            bt = jnp.where(d24 == delta, t, F32(0.0))
            hi = bt.astype(jnp.bfloat16)
            r1 = bt - hi.astype(F32)
            mid = r1.astype(jnp.bfloat16)
            low = (r1 - mid.astype(F32)).astype(jnp.bfloat16)
            rows = lax.broadcasted_iota(jnp.int32, (ny * 128, 512), 0) + ylo * 128
            hot = jnp.where(rows == co, F32(1.0), F32(0.0)).astype(jnp.bfloat16)
            dims = (((1,), (1,)), ((), ()))
            got = lax.dot_general(hi, hot, dims, preferred_element_type=F32)
            got = got + lax.dot_general(mid, hot, dims, preferred_element_type=F32)
            got = got + lax.dot_general(low, hot, dims, preferred_element_type=F32)
            for y in range(ny):
                bands[side, yout + y] = got[:, y * 128 : (y + 1) * 128]

    fd[...] = jnp.zeros((6, 16, 128), F32)
    for side, xs in enumerate((x_own, x_par, x_oth)):
        for y in range(12):
            tile = jnp.zeros((8, 128), F32)
            for d in range(17):
                tile = tile + bands[side, y, d : d + 1, :] * pat[d]
            fp[side, y] = tile
            fd[xs + 2, y + 1 : y + 2, :] = jnp.sum(tile, axis=0, keepdims=True)

    for x in range(-2, 4):
        diag = c_ref[13, x + 3] + wsum[x + 2] + fd[x + 2]
        xg = jnp.full((16, 128), 2 * gx + x, jnp.int32)
        inv = jnp.where(y_in & (xg >= 0) & (xg < 256), 1.0 / diag, F32(0.0))
        diag = jnp.where(y_in & (xg >= 0) & (xg < 256), diag, F32(0.0))
        kf[13, x + 2] = diag
        inv_ref[x + 2] = inv
        for dz in (-1, 0, 1):
            low, high = [], []
            for dx in (-1, 0, 1):
                mid = kf[kid(dx, 0, dz), x + 2]
                low.append(kf[kid(dx, -1, dz), x + 2] + jnp.where(y_odd, mid, F32(0.0)))
                high.append(kf[kid(dx, 1, dz), x + 2] + jnp.where(y_odd, F32(0.0), mid))
            for ry, part in enumerate((low, high)):
                if x % 2:
                    pair = (part[0] + part[1], part[2])
                else:
                    pair = (part[0], part[1] + part[2])
                for rx, total in enumerate(pair):
                    g = inv * total * F32(-damping * tent)
                    if dz == 0 and rx == (0 if x % 2 else 1):
                        mine = y_odd if ry == 0 else jnp.logical_not(y_odd)
                        g = g + jnp.where(mine, F32(tent), F32(0.0))
                    gs[x + 2, rx * 2 + ry, dz + 1] = g

    def smooth(y, carry):
        for x in range(6):
            for r in range(4):
                tile = gs[x, r, 0, pl.ds(y + 1, 1), :] * pat[7]
                tile = tile + gs[x, r, 1, pl.ds(y + 1, 1), :] * pat[8]
                tile = tile + gs[x, r, 2, pl.ds(y + 1, 1), :] * pat[9]
                s3[1, x, y, r] = tile
        ry = 1 - lax.rem(y, 2)
        for side, xs in enumerate((x_own, x_par, x_oth)):
            rx = xs & 1
            iv = inv_ref[xs + 2, pl.ds(y + 1, 1), :] * F32(damping * tent)
            s3[1, xs + 2, y, rx * 2 + ry] += iv * fp[side, y]
        for x in range(6):
            for r in range(4):
                tile = s3[1, x, y, r]
                s3[0, x, y, r] = pltpu.roll(tile, 1, 1)
                s3[2, x, y, r] = pltpu.roll(tile, 127, 1)
        return carry

    lax.fori_loop(0, 12, smooth, 0)

    def apply_pair(t, carry):
        for x in range(-1, 3):
            for p in range(2):
                y = p - 1
                acc = [None] * 9
                for dx in (-1, 0, 1):
                    for dy in (-1, 0, 1):
                        xn, yn = x + dx, y + dy
                        bx = (xn - 1) // 2 - (x // 2 - 1)
                        by = (yn - 1) // 2 - (y // 2 - 1)
                        for dz in (-1, 0, 1):
                            row = kf[kid(dx, dy, dz), x + 2, pl.ds(2 * t + y + 3, 1), :]
                            for rx in range(2):
                                for ry in range(2):
                                    q = (bx + rx) * 3 + by + ry
                                    v = row * s3[dz + 1, xn + 2, 2 * t + yn + 2, rx * 2 + ry]
                                    acc[q] = v if acc[q] is None else acc[q] + v
                for q in range(9):
                    ap[x + 1, 2 * t + y + 1, q] = acc[q]
        return carry

    lax.fori_loop(0, 5, apply_pair, 0)

    def apply_fault(n, carry):
        y = n - 1
        y_is_odd = y & 1
        for side, (xs, xn) in enumerate(((x_own, x_par), (x_par, x_own))):
            for rx in range(2):
                for ry in range(2):
                    tile = s3[1, xn + 2, n + 1, rx * 2 + ry]
                    total = jnp.zeros((8, 128), F32)
                    for d in range(17):
                        row = bands[side, n + 1, d : d + 1, :]
                        total = total + row * pltpu.roll(tile, (8 - d) % 128, 1)
                    q = ((xs & 1) + rx) * 3 + y_is_odd + ry
                    ap[xs + 1, n, q] -= total
        for x in range(4):
            iv = inv_ref[x + 1, pl.ds(n + 2, 1), :]
            for q in range(9):
                tile = ap[x, n, q] * iv
                b3[1, x, n, q] = tile
                b3[0, x, n, q] = pltpu.roll(tile, 1, 1)
                b3[2, x, n, q] = pltpu.roll(tile, 127, 1)
        return carry

    lax.fori_loop(0, 10, apply_fault, 0)

    pz = lax.broadcasted_iota(jnp.int32, (128, 64), 0)
    pc = lax.broadcasted_iota(jnp.int32, (128, 64), 1)
    pick = jnp.where(lax.shift_right_logical(pz, 1) == pc, F32(tent), F32(0.0))

    def restrict(yc, carry):
        acc = [None] * 25
        for xn in range(-1, 3):
            for yn in range(-1, 3):
                bx, by = xn // 2 + 1, yn // 2 + 1
                for dz in (-1, 0, 1):
                    row = None
                    for x in (0, 1):
                        for y in (0, 1):
                            if abs(xn - x) <= 1 and abs(yn - y) <= 1:
                                k = kf[kid(xn - x, yn - y, dz), x + 2, pl.ds(2 * yc + y + 3, 1), :]
                                row = k if row is None else row + k
                    row = row * F32(-damping)
                    if dz == 0 and xn in (0, 1) and yn in (0, 1):
                        row = row + kf[13, xn + 2, pl.ds(2 * yc + yn + 3, 1), :]
                    for rx in range(3):
                        for ry in range(3):
                            q = (bx + rx) * 5 + by + ry
                            v = row * b3[dz + 1, xn + 1, 2 * yc + yn + 1, rx * 3 + ry]
                            acc[q] = v if acc[q] is None else acc[q] + v
        for q in range(25):
            acc_ref[q // 5, q % 5] = acc[q]
        far = lax.shift_right_arithmetic(x_par, 1) + 1
        for rx in range(3):
            for ry in range(3):
                total = jnp.zeros((8, 128), F32)
                for y in range(2):
                    tile = b3[1, x_par + 1, 2 * yc + y + 1, rx * 3 + ry]
                    for d in range(17):
                        row = bands[0, 2 * yc + y + 2, d : d + 1, :]
                        total = total + row * pltpu.roll(tile, (8 - d) % 128, 1)
                acc_ref[far + rx, 1 + ry] += total * F32(damping)
        got = jnp.dot(
            acc_ref[...].reshape(200, 128),
            pick,
            precision=lax.Precision.HIGHEST,
            preferred_element_type=F32,
        )
        for rx in range(5):
            a = lax.rem(gx + rx + 3, 5)
            for ry in range(5):
                b = lax.rem(gy * 4 + yc + ry + 3, 5)
                q = (rx * 5 + ry) * 8
                out_ref[a, b, yc] = got[q : q + 8]
        return carry

    lax.fori_loop(0, 4, restrict, 0)


SOURCES = (
    (-2, 0, 1, 1, 4, 9),
    (-1, 1, 2, 0, 0, 14),
    (0, 3, 2, 0, 0, 14),
    (1, 5, 2, 0, 0, 14),
    (2, None, 0, 0, 0, 0),
)


def exchange(core, fault, wide, slots, send, recv, ysend, yrecv, local):
    gx = lax.axis_index("gx")
    gy = lax.axis_index("gy")

    def has(i):
        return (gx + i >= 0) & (gx + i < 128)

    def has_y(j):
        return (gy + j >= 0) & (gy + j < 4)

    barrier = pltpu.get_barrier_semaphore()
    count = 0
    for i in (-2, -1, 1, 2):
        count = count + has(i).astype(jnp.int32)

        @pl.when(has(i))
        def _(i=i):
            pl.semaphore_signal(
                barrier, inc=1, device_id=(gx + i, gy), device_id_type=pl.DeviceIdType.MESH
            )

    for j in (-1, 1):
        count = count + has_y(j).astype(jnp.int32)

        @pl.when(has_y(j))
        def _(j=j):
            pl.semaphore_signal(
                barrier, inc=1, device_id=(gx, gy + j), device_id_type=pl.DeviceIdType.MESH
            )

    keep = pltpu.make_async_copy(core, wide.at[:, 3:5, 3:11], local.at[0])
    keep.start()
    keep_fault = pltpu.make_async_copy(fault, slots.at[1, 2], local.at[1])
    keep_fault.start()
    pl.semaphore_wait(barrier, count)

    def along_x(n):
        i, x0, nx, own, o0, no = SOURCES[n]
        to = (gx - i, gy)
        copies = []
        if no:
            copies.append(
                pltpu.make_async_remote_copy(
                    core.at[o0 : o0 + no, own : own + nx],
                    wide.at[o0 : o0 + no, x0 : x0 + nx, 3:11],
                    send.at[n, 0],
                    recv.at[n, 0],
                    device_id=to,
                    device_id_type=pl.DeviceIdType.MESH,
                )
            )
        copies.append(
            pltpu.make_async_remote_copy(
                fault,
                slots.at[1, n],
                send.at[n, 1],
                recv.at[n, 1],
                device_id=to,
                device_id_type=pl.DeviceIdType.MESH,
            )
        )
        return copies

    def along_y(n, j):
        i, x0, nx, own, o0, no = SOURCES[n]
        to = (gx, gy + j)
        s = (j + 1) // 2
        y0, y1 = (8, 0) if j == 1 else (3, 11)
        place = 0 if j == 1 else 2
        copies = []
        if no:
            if n == 2:
                source = core.at[:, :, y0 - 3 : y0]
            else:
                source = wide.at[o0 : o0 + no, x0 : x0 + nx, y0 : y0 + 3]
            copies.append(
                pltpu.make_async_remote_copy(
                    source,
                    wide.at[o0 : o0 + no, x0 : x0 + nx, y1 : y1 + 3],
                    ysend.at[s, n, 0],
                    yrecv.at[s, n, 0],
                    device_id=to,
                    device_id_type=pl.DeviceIdType.MESH,
                )
            )
        copies.append(
            pltpu.make_async_remote_copy(
                fault if n == 2 else slots.at[1, n],
                slots.at[place, n],
                ysend.at[s, n, 1],
                yrecv.at[s, n, 1],
                device_id=to,
                device_id_type=pl.DeviceIdType.MESH,
            )
        )
        return copies

    def guarded(ok, copies, what):
        @pl.when(ok)
        def _():
            for c in copies:
                getattr(c, what)()

    for n in (0, 1, 3, 4):
        guarded(has(-SOURCES[n][0]), along_x(n), "start")
    for j in (-1, 1):
        guarded(has_y(j), along_y(2, j), "start")
    for n in (1, 3, 4, 0):
        guarded(has(SOURCES[n][0]), along_x(n), "wait_recv")
        for j in (-1, 1):
            guarded(has(SOURCES[n][0]) & has_y(j), along_y(n, j), "start")
    for n in (0, 1, 3, 4):
        guarded(has(-SOURCES[n][0]), along_x(n), "wait_send")
    for n in range(5):
        for j in (-1, 1):
            guarded(has(SOURCES[n][0]) & has_y(j), along_y(n, j), "wait_send")
            guarded(has(SOURCES[n][0]) & has_y(-j), along_y(n, j), "wait_recv")
    keep.wait()
    keep_fault.wait()


def per_device(trans, storage, fault_cells, fault_count, fault_trans):
    slots = jnp.arange(512, dtype=jnp.int32)
    live = jnp.where(slots < fault_count.reshape(()), fault_trans.reshape(-1), F32(0.0))
    cells = fault_cells.reshape(-1).astype(F32)
    fault = jnp.concatenate([cells.reshape(4, 128), live.reshape(4, 128)], axis=0)
    core = jnp.concatenate(
        [trans.reshape(13, 2, 8, 1, 128), storage.reshape(1, 2, 8, 1, 128)], axis=0
    )
    vm = pl.BlockSpec(memory_space=pltpu.VMEM)
    hbm = pl.BlockSpec(memory_space=pl.ANY)
    wide, faults = pl.pallas_call(
        exchange,
        out_shape=(
            jax.ShapeDtypeStruct((14, 7, 16, 1, 128), F32),
            jax.ShapeDtypeStruct((3, 5, 8, 128), F32),
        ),
        in_specs=[vm, vm],
        out_specs=(hbm, hbm),
        scratch_shapes=[
            pltpu.SemaphoreType.DMA((5, 2)),
            pltpu.SemaphoreType.DMA((5, 2)),
            pltpu.SemaphoreType.DMA((2, 5, 2)),
            pltpu.SemaphoreType.DMA((2, 5, 2)),
            pltpu.SemaphoreType.DMA((2,)),
        ],
        compiler_params=pltpu.CompilerParams(collective_id=0, has_side_effects=True),
    )(core, fault)
    full = wide.reshape(14, 7, 16, 128)
    out = pl.pallas_call(
        body,
        out_shape=jax.ShapeDtypeStruct((5, 5, 4, 8, 64), F32),
        in_specs=[vm, vm],
        out_specs=vm,
        scratch_shapes=[
            pltpu.VMEM((27, 6, 16, 128), F32),
            pltpu.VMEM((6, 16, 128), F32),
            pltpu.VMEM((6, 16, 128), F32),
            pltpu.VMEM((17, 8, 128), F32),
            pltpu.VMEM((3, 12, 24, 128), F32),
            pltpu.VMEM((3, 12, 8, 128), F32),
            pltpu.VMEM((6, 4, 3, 16, 128), F32),
            pltpu.VMEM((3, 6, 12, 4, 8, 128), F32),
            pltpu.VMEM((4, 10, 9, 8, 128), F32),
            pltpu.VMEM((3, 4, 10, 9, 8, 128), F32),
            pltpu.VMEM((5, 5, 8, 128), F32),
        ],
        compiler_params=pltpu.CompilerParams(vmem_limit_bytes=48 * 1024 * 1024),
    )(full, faults)
    return out[:, :, :, :5].transpose(0, 1, 3, 2, 4).reshape(125, 1, 256)


def solution(mesh):
    placed = (
        P(None, "gx", "gy"),
        P("gx", "gy"),
        P("gx", "gy", None),
        P("gx", "gy"),
        P("gx", "gy", None),
    )
    return jax.shard_map(
        per_device, mesh=mesh, in_specs=placed, out_specs=P(None, "gx", "gy"), check_vma=False
    )
```

```python
import jax
import jax.numpy as jnp
from jax import lax
from jax.experimental import pallas as pl
from jax.experimental.pallas import tpu as pltpu
from jax.sharding import PartitionSpec as P

FORWARD = (
    (0, 0, 1),
    (0, 1, -1),
    (0, 1, 0),
    (0, 1, 1),
    (1, -1, -1),
    (1, -1, 0),
    (1, -1, 1),
    (1, 0, -1),
    (1, 0, 0),
    (1, 0, 1),
    (1, 1, -1),
    (1, 1, 0),
    (1, 1, 1),
)
damping = 2.0 / 3.0
tent = 0.35355339059327373
F32 = jnp.float32


def kid(dx, dy, dz):
    return (dx + 1) * 9 + (dy + 1) * 3 + dz + 1


def body(n_any, c_any, fc_any, ft_any, out_ref, counts, c_ref, fc_ref, ft_ref, sems, kf, inv_ref, fd, pat, bands, fp, gs, s3, ap, b3, acc_ref, cols):
    loads = []
    for n, (a, b) in enumerate(
        ((n_any, counts), (fc_any, fc_ref), (ft_any, ft_ref), (c_any, c_ref))
    ):
        loads.append(pltpu.make_async_copy(a, b, sems.at[n]))
        loads[n].start()
    gx = lax.axis_index("gx")
    gy = lax.axis_index("gy")
    odd_dev = lax.rem(gx, 2)
    zl = lax.broadcasted_iota(jnp.int32, (16, 128), 1)
    yi = lax.broadcasted_iota(jnp.int32, (16, 128), 0)
    yg = gy * 8 + yi - 3
    y_in = (yg >= 0) & (yg < 32)
    y_odd = lax.rem(yi, 2) == 0

    e8 = lax.broadcasted_iota(jnp.int32, (8, 128), 0)
    z8 = lax.broadcasted_iota(jnp.int32, (8, 128), 1)
    for d in range(17):
        col = lax.rem(lax.shift_right_logical(z8 + (d - 8 + 160), 1), 5)
        pat[d] = jnp.where(col == e8, F32(1.0), F32(0.0))

    for load in loads:
        load.wait()

    wsum = [jnp.zeros((16, 128), F32) for _ in range(6)]
    for o, (dx, dy, dz) in enumerate(FORWARD):
        ok = y_in & (yg + dy >= 0) & (yg + dy < 32) & (zl + dz >= 0) & (zl + dz < 128)
        for x in range(-3, 4):
            if dx == 0 and x == -3:
                continue
            xg = jnp.full((16, 128), 2 * gx + x, jnp.int32)
            x_ok = (xg >= 0) & (xg + dx < 256)
            m = jnp.where(ok & x_ok, c_ref[o, x + 3], F32(0.0))
            if x >= -2:
                kf[kid(dx, dy, dz), x + 2] = -m
                wsum[x + 2] = wsum[x + 2] + m
            xb = x + dx
            if -2 <= xb <= 3:
                b = m
                if dy:
                    b = pltpu.roll(b, dy % 16, 0)
                if dz:
                    b = pltpu.roll(b, dz % 128, 1)
                kf[kid(-dx, -dy, -dz), xb + 2] = -b
                wsum[xb + 2] = wsum[xb + 2] + b

    x_own = 1 - odd_dev
    x_par = 2 - 3 * odd_dev
    x_oth = 5 * odd_dev - 2
    s_par = 3 - 2 * odd_dev
    s_oth = 1 + 2 * odd_dev
    s_far = 4 * odd_dev
    sides = ((2, s_par, 2), (s_par, 2, 2), (s_oth, s_far, s_oth))

    def slot_row(ref, dev, place):
        return jnp.concatenate([ref[dev, place, i] for i in range(4)], axis=1)

    zrow = lax.broadcasted_iota(jnp.int32, (128, 512), 0)
    slot = lax.broadcasted_iota(jnp.int32, (1, 512), 1)
    for dev, (ylo, ny, yout) in enumerate(((6, 2, 0), (0, 8, 2), (0, 2, 10))):
        for side, (own, par, tr) in enumerate(sides):
            co = slot_row(fc_ref, dev, own) & 1023
            cp = slot_row(fc_ref, dev, par) & 1023
            reach = (gy + dev >= 1) & (gy + dev < 5)
            if side == 2:
                mate = gx + 4 * odd_dev - 2
                reach = reach & (mate >= 0) & (mate < 128)
            count = jnp.concatenate([counts[dev, tr]] * 4, axis=1)
            alive = jnp.where(jnp.full((1, 512), reach.astype(jnp.int32)) > 0, count, 0)
            t = jnp.where(slot < alive, slot_row(ft_ref, dev, tr), F32(0.0))
            zo = co & 127
            key = (lax.shift_right_logical(co, 7) - ylo) * 24 + (cp & 127) - zo + 8
            hit = lax.broadcasted_iota(jnp.int32, (ny * 24, 512), 0) == key
            hi = t.astype(jnp.bfloat16).astype(F32)
            mid = (t - hi).astype(jnp.bfloat16).astype(F32)
            parts = [
                jnp.where(hit, p, F32(0.0)).astype(jnp.bfloat16) for p in (hi, mid, t - hi - mid)
            ]
            hot = jnp.where(zrow == zo, F32(1.0), F32(0.0)).astype(jnp.bfloat16)
            got = lax.dot_general(
                jnp.concatenate(parts, axis=0),
                hot,
                (((1,), (1,)), ((), ())),
                preferred_element_type=F32,
            )
            n = ny * 24
            got = got[:n] + got[n : 2 * n] + got[2 * n :]
            bands[side, yout : yout + ny] = got.reshape(ny, 24, 128)

    fd[...] = jnp.zeros((6, 16, 128), F32)
    for side, xs in enumerate((x_own, x_par, x_oth)):
        for y in range(12):
            tile = jnp.zeros((8, 128), F32)
            for d in range(17):
                tile = tile + bands[side, y, d : d + 1, :] * pat[d]
            fp[side, y] = tile
            fd[xs + 2, y + 1 : y + 2, :] = jnp.sum(tile, axis=0, keepdims=True)

    for x in range(-2, 4):
        diag = c_ref[13, x + 3] + wsum[x + 2] + fd[x + 2]
        xg = jnp.full((16, 128), 2 * gx + x, jnp.int32)
        inv = jnp.where(y_in & (xg >= 0) & (xg < 256), 1.0 / diag, F32(0.0))
        diag = jnp.where(y_in & (xg >= 0) & (xg < 256), diag, F32(0.0))
        kf[13, x + 2] = diag
        inv_ref[x + 2] = inv
        for dz in (-1, 0, 1):
            low, high = [], []
            for dx in (-1, 0, 1):
                mid = kf[kid(dx, 0, dz), x + 2]
                low.append(kf[kid(dx, -1, dz), x + 2] + jnp.where(y_odd, mid, F32(0.0)))
                high.append(kf[kid(dx, 1, dz), x + 2] + jnp.where(y_odd, F32(0.0), mid))
            for ry, part in enumerate((low, high)):
                if x % 2:
                    pair = (part[0] + part[1], part[2])
                else:
                    pair = (part[0], part[1] + part[2])
                for rx, total in enumerate(pair):
                    g = inv * total * F32(-damping * tent)
                    if dz == 0 and rx == (0 if x % 2 else 1):
                        mine = y_odd if ry == 0 else jnp.logical_not(y_odd)
                        g = g + jnp.where(mine, F32(tent), F32(0.0))
                    gs[x + 2, rx * 2 + ry, dz + 1] = g

    def smooth(y, carry):
        for x in range(6):
            for r in range(4):
                tile = gs[x, r, 0, pl.ds(y + 1, 1), :] * pat[7]
                tile = tile + gs[x, r, 1, pl.ds(y + 1, 1), :] * pat[8]
                tile = tile + gs[x, r, 2, pl.ds(y + 1, 1), :] * pat[9]
                s3[1, x, y, r] = tile
        ry = 1 - lax.rem(y, 2)
        for side, xs in enumerate((x_own, x_par, x_oth)):
            rx = xs & 1
            iv = inv_ref[xs + 2, pl.ds(y + 1, 1), :] * F32(damping * tent)
            s3[1, xs + 2, y, rx * 2 + ry] += iv * fp[side, y]
        for x in range(6):
            for r in range(4):
                tile = s3[1, x, y, r]
                s3[0, x, y, r] = pltpu.roll(tile, 1, 1)
                s3[2, x, y, r] = pltpu.roll(tile, 127, 1)
        return carry

    lax.fori_loop(0, 12, smooth, 0)

    def apply_pair(t, carry):
        for x in range(-1, 3):
            for p in range(2):
                y = p - 1
                acc = [None] * 9
                for dx in (-1, 0, 1):
                    for dy in (-1, 0, 1):
                        xn, yn = x + dx, y + dy
                        bx = (xn - 1) // 2 - (x // 2 - 1)
                        by = (yn - 1) // 2 - (y // 2 - 1)
                        for dz in (-1, 0, 1):
                            row = kf[kid(dx, dy, dz), x + 2, pl.ds(2 * t + y + 3, 1), :]
                            for rx in range(2):
                                for ry in range(2):
                                    q = (bx + rx) * 3 + by + ry
                                    v = row * s3[dz + 1, xn + 2, 2 * t + yn + 2, rx * 2 + ry]
                                    acc[q] = v if acc[q] is None else acc[q] + v
                for q in range(9):
                    ap[x + 1, 2 * t + y + 1, q] = acc[q]
        return carry

    lax.fori_loop(0, 5, apply_pair, 0)

    def apply_fault(n, carry):
        y = n - 1
        y_is_odd = y & 1
        for side, (xs, xn) in enumerate(((x_own, x_par), (x_par, x_own))):
            for rx in range(2):
                for ry in range(2):
                    tile = s3[1, xn + 2, n + 1, rx * 2 + ry]
                    total = jnp.zeros((8, 128), F32)
                    for d in range(17):
                        row = bands[side, n + 1, d : d + 1, :]
                        total = total + row * pltpu.roll(tile, (8 - d) % 128, 1)
                    q = ((xs & 1) + rx) * 3 + y_is_odd + ry
                    ap[xs + 1, n, q] -= total
        for x in range(4):
            iv = inv_ref[x + 1, pl.ds(n + 2, 1), :]
            for q in range(9):
                tile = ap[x, n, q] * iv
                b3[1, x, n, q] = tile
                b3[0, x, n, q] = pltpu.roll(tile, 1, 1)
                b3[2, x, n, q] = pltpu.roll(tile, 127, 1)
        return carry

    lax.fori_loop(0, 10, apply_fault, 0)

    pz = lax.broadcasted_iota(jnp.int32, (128, 64), 0)
    pc = lax.broadcasted_iota(jnp.int32, (128, 64), 1)
    pick = jnp.where(lax.shift_right_logical(pz, 1) == pc, F32(tent), F32(0.0))

    def restrict(yc, carry):
        acc = [None] * 25
        for xn in range(-1, 3):
            for yn in range(-1, 3):
                bx, by = xn // 2 + 1, yn // 2 + 1
                for dz in (-1, 0, 1):
                    row = None
                    for x in (0, 1):
                        for y in (0, 1):
                            if abs(xn - x) <= 1 and abs(yn - y) <= 1:
                                k = kf[kid(xn - x, yn - y, dz), x + 2, pl.ds(2 * yc + y + 3, 1), :]
                                row = k if row is None else row + k
                    row = row * F32(-damping)
                    if dz == 0 and xn in (0, 1) and yn in (0, 1):
                        row = row + kf[13, xn + 2, pl.ds(2 * yc + yn + 3, 1), :]
                    for rx in range(3):
                        for ry in range(3):
                            q = (bx + rx) * 5 + by + ry
                            v = row * b3[dz + 1, xn + 1, 2 * yc + yn + 1, rx * 3 + ry]
                            acc[q] = v if acc[q] is None else acc[q] + v
        for q in range(25):
            acc_ref[q // 5, q % 5] = acc[q]
        far = lax.shift_right_arithmetic(x_par, 1) + 1
        for rx in range(3):
            for ry in range(3):
                total = jnp.zeros((8, 128), F32)
                for y in range(2):
                    tile = b3[1, x_par + 1, 2 * yc + y + 1, rx * 3 + ry]
                    for d in range(17):
                        row = bands[0, 2 * yc + y + 2, d : d + 1, :]
                        total = total + row * pltpu.roll(tile, (8 - d) % 128, 1)
                acc_ref[far + rx, 1 + ry] += total * F32(damping)
        got = jnp.dot(
            acc_ref[...].reshape(200, 128),
            pick,
            precision=lax.Precision.HIGHEST,
            preferred_element_type=F32,
        )
        for rx in range(5):
            a = lax.rem(gx + rx + 3, 5)
            for ry in range(5):
                b = lax.rem(gy * 4 + yc + ry + 3, 5)
                q = (rx * 5 + ry) * 8
                cols[a, b, yc] = got[q : q + 8]
        return carry

    lax.fori_loop(0, 4, restrict, 0)
    for a in range(5):
        for b in range(5):
            tile = jnp.concatenate([cols[a, b, yc] for yc in range(4)], axis=1)
            c = (a * 5 + b) * 5
            out_ref[c : c + 5, 0, :] = tile[:5]


SOURCES = (
    (-2, 0, 1, 1, 4, 9),
    (-1, 1, 2, 0, 0, 14),
    (0, 3, 2, 0, 0, 14),
    (1, 5, 2, 0, 0, 14),
    (2, None, 0, 0, 0, 0),
)


def exchange(trans, storage, cells, weights, count, wide, slot_c, slot_t, slot_n, send, recv, ysend, yrecv, local):
    gx = lax.axis_index("gx")
    gy = lax.axis_index("gy")

    def has(i):
        return (gx + i >= 0) & (gx + i < 128)

    def has_y(j):
        return (gy + j >= 0) & (gy + j < 4)

    barrier = pltpu.get_barrier_semaphore()
    count_in = 0
    for i in (-2, -1, 1, 2):
        count_in = count_in + has(i).astype(jnp.int32)

        @pl.when(has(i))
        def _(i=i):
            pl.semaphore_signal(
                barrier, inc=1, device_id=(gx + i, gy), device_id_type=pl.DeviceIdType.MESH
            )

    for j in (-1, 1):
        count_in = count_in + has_y(j).astype(jnp.int32)

        @pl.when(has_y(j))
        def _(j=j):
            pl.semaphore_signal(
                barrier, inc=1, device_id=(gx, gy + j), device_id_type=pl.DeviceIdType.MESH
            )

    def faults(n):
        return ((cells, slot_c, n), (weights, slot_t, n), (count, slot_n, n))

    keeps = []
    for x in range(2):
        keeps.append((trans.at[:, :, x], wide.at[0:13, 3 + x, 3:11]))
        keeps.append((storage.at[:, x], wide.at[13, 3 + x, 3:11]))
    for own, slots, n in faults(2):
        keeps.append((own, slots.at[1, n]))
    keeps = [pltpu.make_async_copy(a, b, local.at[n]) for n, (a, b) in enumerate(keeps)]
    for k in keeps:
        k.start()
    pl.semaphore_wait(barrier, count_in)

    def remote(pairs, sends, recvs, to):
        return [
            pltpu.make_async_remote_copy(
                a,
                b,
                sends.at[k],
                recvs.at[k],
                device_id=to,
                device_id_type=pl.DeviceIdType.MESH,
            )
            for k, (a, b) in enumerate(pairs)
        ]

    def along_x(n):
        i, x0, nx, own, o0, no = SOURCES[n]
        pairs = []
        for x in range(nx):
            last = min(o0 + no, 13)
            pairs.append((trans.at[o0:last, :, own + x], wide.at[o0:last, x0 + x, 3:11]))
            if no == 14:
                pairs.append((storage.at[:, own + x], wide.at[13, x0 + x, 3:11]))
        pairs += [(a, slots.at[1, m]) for a, slots, m in faults(n)]
        return remote(pairs, send.at[n], recv.at[n], (gx - i, gy))

    def along_y(n, j):
        i, x0, nx, own, o0, no = SOURCES[n]
        y0, y1 = (8, 0) if j == 1 else (3, 11)
        place = 0 if j == 1 else 2
        pairs = []
        if n == 2:
            for x in range(2):
                pairs.append(
                    (trans.at[:, y0 - 3 : y0, x], wide.at[0:13, 3 + x, y1 : y1 + 3])
                )
                pairs.append((storage.at[y0 - 3 : y0, x], wide.at[13, 3 + x, y1 : y1 + 3]))
        elif no:
            cut = wide.at[o0 : o0 + no, x0 : x0 + nx]
            pairs.append((cut.at[:, :, y0 : y0 + 3], cut.at[:, :, y1 : y1 + 3]))
        for a, slots, m in faults(n):
            pairs.append((a if n == 2 else slots.at[1, m], slots.at[place, m]))
        s = (j + 1) // 2
        return remote(pairs, ysend.at[s, n], yrecv.at[s, n], (gx, gy + j))

    def guarded(ok, copies, what):
        @pl.when(ok)
        def _():
            for c in copies:
                getattr(c, what)()

    for n in (0, 1, 3, 4):
        guarded(has(-SOURCES[n][0]), along_x(n), "start")
    for j in (-1, 1):
        guarded(has_y(j), along_y(2, j), "start")
    for n in (1, 3, 4, 0):
        guarded(has(SOURCES[n][0]), along_x(n), "wait_recv")
        for j in (-1, 1):
            guarded(has(SOURCES[n][0]) & has_y(j), along_y(n, j), "start")
    for n in (0, 1, 3, 4):
        guarded(has(-SOURCES[n][0]), along_x(n), "wait_send")
    for n in range(5):
        for j in (-1, 1):
            guarded(has(SOURCES[n][0]) & has_y(j), along_y(n, j), "wait_send")
            guarded(has(SOURCES[n][0]) & has_y(-j), along_y(n, j), "wait_recv")
    for k in keeps:
        k.wait()


def per_device(trans, storage, fault_cells, fault_count, fault_trans):
    any_space = pl.BlockSpec(memory_space=pltpu.HBM)
    wide, slot_c, slot_t, slot_n = pl.pallas_call(
        exchange,
        out_shape=(
            jax.ShapeDtypeStruct((14, 7, 16, 1, 128), F32),
            jax.ShapeDtypeStruct((3, 5, 4, 1, 128), jnp.int32),
            jax.ShapeDtypeStruct((3, 5, 4, 1, 128), F32),
            jax.ShapeDtypeStruct((3, 5, 1, 128), jnp.int32),
        ),
        in_specs=[any_space] * 5,
        out_specs=(any_space,) * 4,
        scratch_shapes=[
            pltpu.SemaphoreType.DMA((5, 7)),
            pltpu.SemaphoreType.DMA((5, 7)),
            pltpu.SemaphoreType.DMA((2, 5, 7)),
            pltpu.SemaphoreType.DMA((2, 5, 7)),
            pltpu.SemaphoreType.DMA((7,)),
        ],
        compiler_params=pltpu.CompilerParams(
            collective_id=0, has_side_effects=True, vmem_limit_bytes=67043328
        ),
    )(
        trans.reshape(13, 2, 8, 128).transpose(0, 2, 1, 3).reshape(13, 8, 2, 1, 128),
        storage.reshape(2, 8, 128).transpose(1, 0, 2).reshape(8, 2, 1, 128),
        fault_cells.reshape(4, 1, 128),
        fault_trans.reshape(4, 1, 128),
        jnp.broadcast_to(fault_count.reshape(1, 1), (1, 128)),
    )
    return pl.pallas_call(
        body,
        out_shape=jax.ShapeDtypeStruct((125, 1, 256), F32),
        in_specs=[any_space] * 4,
        out_specs=pl.BlockSpec(memory_space=pltpu.VMEM),
        scratch_shapes=[
            pltpu.VMEM((3, 5, 1, 128), jnp.int32),
            pltpu.VMEM((14, 7, 16, 128), F32),
            pltpu.VMEM((3, 5, 4, 1, 128), jnp.int32),
            pltpu.VMEM((3, 5, 4, 1, 128), F32),
            pltpu.SemaphoreType.DMA((4,)),
            pltpu.VMEM((27, 6, 16, 128), F32),
            pltpu.VMEM((6, 16, 128), F32),
            pltpu.VMEM((6, 16, 128), F32),
            pltpu.VMEM((17, 8, 128), F32),
            pltpu.VMEM((3, 12, 24, 128), F32),
            pltpu.VMEM((3, 12, 8, 128), F32),
            pltpu.VMEM((6, 4, 3, 16, 128), F32),
            pltpu.VMEM((3, 6, 12, 4, 8, 128), F32),
            pltpu.VMEM((4, 10, 9, 8, 128), F32),
            pltpu.VMEM((3, 4, 10, 9, 8, 128), F32),
            pltpu.VMEM((5, 5, 8, 128), F32),
            pltpu.VMEM((5, 5, 4, 8, 64), F32),
        ],
        compiler_params=pltpu.CompilerParams(vmem_limit_bytes=67043328),
    )(slot_n, wide.reshape(14, 7, 16, 128), slot_c, slot_t)


def solution(mesh):
    placed = (
        P(None, "gx", "gy"),
        P("gx", "gy"),
        P("gx", "gy", None),
        P("gx", "gy"),
        P("gx", "gy", None),
    )
    return jax.shard_map(
        per_device, mesh=mesh, in_specs=placed, out_specs=P(None, "gx", "gy"), check_vma=False
    )
```

```python
import jax
import jax.numpy as jnp
from jax import lax
from jax.experimental import pallas as pl
from jax.experimental.pallas import tpu as pltpu
from jax.sharding import PartitionSpec as P

FORWARD = (
    (0, 0, 1),
    (0, 1, -1),
    (0, 1, 0),
    (0, 1, 1),
    (1, -1, -1),
    (1, -1, 0),
    (1, -1, 1),
    (1, 0, -1),
    (1, 0, 0),
    (1, 0, 1),
    (1, 1, -1),
    (1, 1, 0),
    (1, 1, 1),
)
damping = 2.0 / 3.0
tent = 0.35355339059327373
F32 = jnp.float32


def kid(dx, dy, dz):
    return (dx + 1) * 9 + (dy + 1) * 3 + dz + 1


def body(n_any, c_any, fc_any, ft_any, out_ref, counts, c_ref, fc_ref, ft_ref, sems, kf, inv_ref, fd, pat, bands, fp, gs, s3, b3, acc_ref, cols):
    loads = []
    for n, (a, b) in enumerate(
        ((n_any, counts), (fc_any, fc_ref), (ft_any, ft_ref), (c_any, c_ref))
    ):
        loads.append(pltpu.make_async_copy(a, b, sems.at[n]))
        loads[n].start()
    gx = lax.axis_index("gx")
    gy = lax.axis_index("gy")
    odd_dev = lax.rem(gx, 2)
    zl = lax.broadcasted_iota(jnp.int32, (16, 128), 1)
    yi = lax.broadcasted_iota(jnp.int32, (16, 128), 0)
    yg = gy * 8 + yi - 3
    y_in = (yg >= 0) & (yg < 32)
    y_odd = lax.rem(yi, 2) == 0

    e8 = lax.broadcasted_iota(jnp.int32, (8, 128), 0)
    z8 = lax.broadcasted_iota(jnp.int32, (8, 128), 1)
    for d in range(17):
        col = lax.rem(lax.shift_right_logical(z8 + (d - 8 + 160), 1), 5)
        pat[d] = jnp.where(col == e8, F32(1.0), F32(0.0))

    for load in loads:
        load.wait()

    wsum = [jnp.zeros((16, 128), F32) for _ in range(6)]
    for o, (dx, dy, dz) in enumerate(FORWARD):
        ok = y_in & (yg + dy >= 0) & (yg + dy < 32) & (zl + dz >= 0) & (zl + dz < 128)
        for x in range(-3, 4):
            if dx == 0 and x == -3:
                continue
            xg = jnp.full((16, 128), 2 * gx + x, jnp.int32)
            x_ok = (xg >= 0) & (xg + dx < 256)
            m = jnp.where(ok & x_ok, c_ref[o, x + 3], F32(0.0))
            if x >= -2:
                kf[kid(dx, dy, dz), x + 2] = -m
                wsum[x + 2] = wsum[x + 2] + m
            xb = x + dx
            if -2 <= xb <= 3:
                b = m
                if dy:
                    b = pltpu.roll(b, dy % 16, 0)
                if dz:
                    b = pltpu.roll(b, dz % 128, 1)
                kf[kid(-dx, -dy, -dz), xb + 2] = -b
                wsum[xb + 2] = wsum[xb + 2] + b

    x_own = 1 - odd_dev
    x_par = 2 - 3 * odd_dev
    x_oth = 5 * odd_dev - 2
    s_par = 3 - 2 * odd_dev
    s_oth = 1 + 2 * odd_dev
    s_far = 4 * odd_dev
    sides = ((2, s_par, 2), (s_par, 2, 2), (s_oth, s_far, s_oth))

    def slot_row(ref, dev, place):
        return jnp.concatenate([ref[dev, place, i] for i in range(4)], axis=1)

    zrow = lax.broadcasted_iota(jnp.int32, (128, 512), 0)
    slot = lax.broadcasted_iota(jnp.int32, (1, 512), 1)
    for dev, (ylo, ny, yout) in enumerate(((6, 2, 0), (0, 8, 2), (0, 2, 10))):
        for side, (own, par, tr) in enumerate(sides):
            co = slot_row(fc_ref, dev, own) & 1023
            cp = slot_row(fc_ref, dev, par) & 1023
            reach = (gy + dev >= 1) & (gy + dev < 5)
            if side == 2:
                mate = gx + 4 * odd_dev - 2
                reach = reach & (mate >= 0) & (mate < 128)
            count = jnp.concatenate([counts[dev, tr]] * 4, axis=1)
            alive = jnp.where(jnp.full((1, 512), reach.astype(jnp.int32)) > 0, count, 0)
            t = jnp.where(slot < alive, slot_row(ft_ref, dev, tr), F32(0.0))
            zo = co & 127
            key = (lax.shift_right_logical(co, 7) - ylo) * 24 + (cp & 127) - zo + 8
            hit = lax.broadcasted_iota(jnp.int32, (ny * 24, 512), 0) == key
            hi = t.astype(jnp.bfloat16).astype(F32)
            mid = (t - hi).astype(jnp.bfloat16).astype(F32)
            parts = [
                jnp.where(hit, p, F32(0.0)).astype(jnp.bfloat16) for p in (hi, mid, t - hi - mid)
            ]
            hot = jnp.where(zrow == zo, F32(1.0), F32(0.0)).astype(jnp.bfloat16)
            got = lax.dot_general(
                jnp.concatenate(parts, axis=0),
                hot,
                (((1,), (1,)), ((), ())),
                preferred_element_type=F32,
            )
            n = ny * 24
            got = got[:n] + got[n : 2 * n] + got[2 * n :]
            bands[side, yout : yout + ny] = got.reshape(ny, 24, 128)

    fd[...] = jnp.zeros((6, 16, 128), F32)
    for side, xs in enumerate((x_own, x_par, x_oth)):
        for y in range(12):
            tile = jnp.zeros((8, 128), F32)
            for d in range(17):
                tile = tile + bands[side, y, d : d + 1, :] * pat[d]
            fp[side, y] = tile
            fd[xs + 2, y + 1 : y + 2, :] = jnp.sum(tile, axis=0, keepdims=True)

    for x in range(-2, 4):
        diag = c_ref[13, x + 3] + wsum[x + 2] + fd[x + 2]
        xg = jnp.full((16, 128), 2 * gx + x, jnp.int32)
        inv = jnp.where(y_in & (xg >= 0) & (xg < 256), 1.0 / diag, F32(0.0))
        diag = jnp.where(y_in & (xg >= 0) & (xg < 256), diag, F32(0.0))
        kf[13, x + 2] = diag
        inv_ref[x + 2] = inv
        for dz in (-1, 0, 1):
            low, high = [], []
            for dx in (-1, 0, 1):
                mid = kf[kid(dx, 0, dz), x + 2]
                low.append(kf[kid(dx, -1, dz), x + 2] + jnp.where(y_odd, mid, F32(0.0)))
                high.append(kf[kid(dx, 1, dz), x + 2] + jnp.where(y_odd, F32(0.0), mid))
            for ry, part in enumerate((low, high)):
                if x % 2:
                    pair = (part[0] + part[1], part[2])
                else:
                    pair = (part[0], part[1] + part[2])
                for rx, total in enumerate(pair):
                    g = inv * total * F32(-damping * tent)
                    if dz == 0 and rx == (0 if x % 2 else 1):
                        mine = y_odd if ry == 0 else jnp.logical_not(y_odd)
                        g = g + jnp.where(mine, F32(tent), F32(0.0))
                    gs[x + 2, rx * 2 + ry, dz + 1] = g

    def smooth(y, carry):
        for x in range(6):
            for r in range(4):
                tile = gs[x, r, 0, pl.ds(y + 1, 1), :] * pat[7]
                tile = tile + gs[x, r, 1, pl.ds(y + 1, 1), :] * pat[8]
                tile = tile + gs[x, r, 2, pl.ds(y + 1, 1), :] * pat[9]
                s3[1, x, y, r] = tile
                s3[0, x, y, r] = pltpu.roll(tile, 1, 1)
                s3[2, x, y, r] = pltpu.roll(tile, 127, 1)
        ry = 1 - lax.rem(y, 2)
        for side, xs in enumerate((x_own, x_par, x_oth)):
            rx = xs & 1
            iv = inv_ref[xs + 2, pl.ds(y + 1, 1), :] * F32(damping * tent)
            tile = s3[1, xs + 2, y, rx * 2 + ry] + iv * fp[side, y]
            s3[1, xs + 2, y, rx * 2 + ry] = tile
            s3[0, xs + 2, y, rx * 2 + ry] = pltpu.roll(tile, 1, 1)
            s3[2, xs + 2, y, rx * 2 + ry] = pltpu.roll(tile, 127, 1)
        return carry

    lax.fori_loop(0, 12, smooth, 0, unroll=2)

    def apply_pair(t, carry):
        for x in range(-1, 3):
            for p in range(2):
                y = p - 1
                acc = [None] * 9
                for dx in (-1, 0, 1):
                    for dy in (-1, 0, 1):
                        xn, yn = x + dx, y + dy
                        bx = (xn - 1) // 2 - (x // 2 - 1)
                        by = (yn - 1) // 2 - (y // 2 - 1)
                        for dz in (-1, 0, 1):
                            row = kf[kid(dx, dy, dz), x + 2, pl.ds(2 * t + y + 3, 1), :]
                            for rx in range(2):
                                for ry in range(2):
                                    q = (bx + rx) * 3 + by + ry
                                    v = row * s3[dz + 1, xn + 2, 2 * t + yn + 2, rx * 2 + ry]
                                    acc[q] = v if acc[q] is None else acc[q] + v
                iv = inv_ref[x + 2, pl.ds(2 * t + y + 3, 1), :]
                for q in range(9):
                    tile = acc[q] * iv
                    b3[x + 1, 2 * t + y + 1, q] = tile
        return carry

    lax.fori_loop(0, 5, apply_pair, 0)

    def apply_fault(n, carry):
        y_is_odd = (n - 1) & 1
        for side, (xs, xn) in enumerate(((x_own, x_par), (x_par, x_own))):
            iv = inv_ref[xs + 2, pl.ds(n + 2, 1), :]
            done = []
            for r in range(4):
                tile = s3[1, xn + 2, n + 1, r]
                total = jnp.zeros((8, 128), F32)
                for d in range(17):
                    row = bands[side, n + 1, d : d + 1, :]
                    total = total + row * pltpu.roll(tile, (8 - d) % 128, 1)
                q = ((xs & 1) + r // 2) * 3 + y_is_odd + r % 2
                done.append((q, b3[xs + 1, n, q] - total * iv))
            for q, tile in done:
                b3[xs + 1, n, q] = tile
        return carry

    lax.fori_loop(0, 10, apply_fault, 0, unroll=2)

    pz = lax.broadcasted_iota(jnp.int32, (128, 64), 0)
    pc = lax.broadcasted_iota(jnp.int32, (128, 64), 1)
    pick = jnp.where(lax.shift_right_logical(pz, 1) == pc, F32(tent), F32(0.0))

    def restrict(yc, carry):
        for dz in (-1, 1, 0):
            acc = [None] * 25
            for xn in range(-1, 3):
                for yn in range(-1, 3):
                    bx, by = xn // 2 + 1, yn // 2 + 1
                    row = None
                    for x in (0, 1):
                        for y in (0, 1):
                            if abs(xn - x) <= 1 and abs(yn - y) <= 1:
                                k = kf[kid(xn - x, yn - y, dz), x + 2, pl.ds(2 * yc + y + 3, 1), :]
                                row = k if row is None else row + k
                    row = row * F32(-damping)
                    if dz == 0 and xn in (0, 1) and yn in (0, 1):
                        row = row + kf[13, xn + 2, pl.ds(2 * yc + yn + 3, 1), :]
                    row = jnp.broadcast_to(row, (8, 128))
                    if dz:
                        row = pltpu.roll(row, dz % 128, 1)
                    for rx in range(3):
                        for ry in range(3):
                            q = (bx + rx) * 5 + by + ry
                            v = row * b3[xn + 1, 2 * yc + yn + 1, rx * 3 + ry]
                            acc[q] = v if acc[q] is None else acc[q] + v
            for q in range(25):
                v = pltpu.roll(acc[q], -dz % 128, 1) if dz else acc[q]
                acc_ref[yc, q // 5, q % 5] = v if dz == -1 else acc_ref[yc, q // 5, q % 5] + v
        far = lax.shift_right_arithmetic(x_par, 1) + 1
        for rx in range(3):
            for ry in range(3):
                total = jnp.zeros((8, 128), F32)
                for y in range(2):
                    tile = b3[x_par + 1, 2 * yc + y + 1, rx * 3 + ry]
                    for d in range(17):
                        row = bands[0, 2 * yc + y + 2, d : d + 1, :]
                        total = total + row * pltpu.roll(tile, (8 - d) % 128, 1)
                acc_ref[yc, far + rx, 1 + ry] += total * F32(damping)
        return carry

    lax.fori_loop(0, 4, restrict, 0)
    got = jnp.dot(
        acc_ref[...].reshape(800, 128),
        pick,
        precision=lax.Precision.HIGHEST,
        preferred_element_type=F32,
    )
    for yc in range(4):
        for rx in range(5):
            a = lax.rem(gx + rx + 3, 5)
            for ry in range(5):
                b = lax.rem(gy * 4 + yc + ry + 3, 5)
                q = (yc * 25 + rx * 5 + ry) * 8
                cols[a, b, yc] = got[q : q + 8]
    for a in range(5):
        for b in range(5):
            tile = jnp.concatenate([cols[a, b, yc] for yc in range(4)], axis=1)
            c = (a * 5 + b) * 5
            out_ref[c : c + 5, 0, :] = tile[:5]


SOURCES = (
    (-2, 0, 1, 1, 4, 9),
    (-1, 1, 2, 0, 0, 14),
    (0, 3, 2, 0, 0, 14),
    (1, 5, 2, 0, 0, 14),
    (2, None, 0, 0, 0, 0),
)


def exchange(trans, storage, cells, weights, count, wide, slot_c, slot_t, slot_n, send, recv, ysend, yrecv, local):
    gx = lax.axis_index("gx")
    gy = lax.axis_index("gy")

    def has(i):
        return (gx + i >= 0) & (gx + i < 128)

    def has_y(j):
        return (gy + j >= 0) & (gy + j < 4)

    barrier = pltpu.get_barrier_semaphore()
    count_in = 0
    for i in (-2, -1, 1, 2):
        count_in = count_in + has(i).astype(jnp.int32)

        @pl.when(has(i))
        def _(i=i):
            pl.semaphore_signal(
                barrier, inc=1, device_id=(gx + i, gy), device_id_type=pl.DeviceIdType.MESH
            )

    for j in (-1, 1):
        count_in = count_in + has_y(j).astype(jnp.int32)

        @pl.when(has_y(j))
        def _(j=j):
            pl.semaphore_signal(
                barrier, inc=1, device_id=(gx, gy + j), device_id_type=pl.DeviceIdType.MESH
            )

    def faults(n):
        return ((cells, slot_c, n), (weights, slot_t, n), (count, slot_n, n))

    keeps = []
    for x in range(2):
        keeps.append((trans.at[:, :, x], wide.at[0:13, 3 + x, 3:11]))
        keeps.append((storage.at[:, x], wide.at[13, 3 + x, 3:11]))
    for own, slots, n in faults(2):
        keeps.append((own, slots.at[1, n]))
    keeps = [pltpu.make_async_copy(a, b, local.at[n]) for n, (a, b) in enumerate(keeps)]
    for k in keeps:
        k.start()
    pl.semaphore_wait(barrier, count_in)

    def remote(pairs, sends, recvs, to):
        return [
            pltpu.make_async_remote_copy(
                a,
                b,
                sends.at[k],
                recvs.at[k],
                device_id=to,
                device_id_type=pl.DeviceIdType.MESH,
            )
            for k, (a, b) in enumerate(pairs)
        ]

    def along_x(n):
        i, x0, nx, own, o0, no = SOURCES[n]
        pairs = []
        for x in range(nx):
            last = min(o0 + no, 13)
            pairs.append((trans.at[o0:last, :, own + x], wide.at[o0:last, x0 + x, 3:11]))
            if no == 14:
                pairs.append((storage.at[:, own + x], wide.at[13, x0 + x, 3:11]))
        pairs += [(a, slots.at[1, m]) for a, slots, m in faults(n)]
        return remote(pairs, send.at[n], recv.at[n], (gx - i, gy))

    def along_y(n, j):
        i, x0, nx, own, o0, no = SOURCES[n]
        y0, y1 = (8, 0) if j == 1 else (3, 11)
        place = 0 if j == 1 else 2
        pairs = []
        if n == 2:
            for x in range(2):
                pairs.append(
                    (trans.at[:, y0 - 3 : y0, x], wide.at[0:13, 3 + x, y1 : y1 + 3])
                )
                pairs.append((storage.at[y0 - 3 : y0, x], wide.at[13, 3 + x, y1 : y1 + 3]))
        elif no:
            cut = wide.at[o0 : o0 + no, x0 : x0 + nx]
            pairs.append((cut.at[:, :, y0 : y0 + 3], cut.at[:, :, y1 : y1 + 3]))
        for a, slots, m in faults(n):
            pairs.append((a if n == 2 else slots.at[1, m], slots.at[place, m]))
        s = (j + 1) // 2
        return remote(pairs, ysend.at[s, n], yrecv.at[s, n], (gx, gy + j))

    def guarded(ok, copies, what):
        @pl.when(ok)
        def _():
            for c in copies:
                getattr(c, what)()

    for n in (0, 1, 3, 4):
        guarded(has(-SOURCES[n][0]), along_x(n), "start")
    for j in (-1, 1):
        guarded(has_y(j), along_y(2, j), "start")
    for n in (1, 3, 4, 0):
        guarded(has(SOURCES[n][0]), along_x(n), "wait_recv")
        for j in (-1, 1):
            guarded(has(SOURCES[n][0]) & has_y(j), along_y(n, j), "start")
    for n in (0, 1, 3, 4):
        guarded(has(-SOURCES[n][0]), along_x(n), "wait_send")
    for n in range(5):
        for j in (-1, 1):
            guarded(has(SOURCES[n][0]) & has_y(j), along_y(n, j), "wait_send")
            guarded(has(SOURCES[n][0]) & has_y(-j), along_y(n, j), "wait_recv")
    for k in keeps:
        k.wait()


def per_device(trans, storage, fault_cells, fault_count, fault_trans):
    any_space = pl.BlockSpec(memory_space=pltpu.HBM)
    wide, slot_c, slot_t, slot_n = pl.pallas_call(
        exchange,
        out_shape=(
            jax.ShapeDtypeStruct((14, 7, 16, 1, 128), F32),
            jax.ShapeDtypeStruct((3, 5, 4, 1, 128), jnp.int32),
            jax.ShapeDtypeStruct((3, 5, 4, 1, 128), F32),
            jax.ShapeDtypeStruct((3, 5, 1, 128), jnp.int32),
        ),
        in_specs=[any_space] * 5,
        out_specs=(any_space,) * 4,
        scratch_shapes=[
            pltpu.SemaphoreType.DMA((5, 7)),
            pltpu.SemaphoreType.DMA((5, 7)),
            pltpu.SemaphoreType.DMA((2, 5, 7)),
            pltpu.SemaphoreType.DMA((2, 5, 7)),
            pltpu.SemaphoreType.DMA((7,)),
        ],
        compiler_params=pltpu.CompilerParams(
            collective_id=0, has_side_effects=True, vmem_limit_bytes=67043328
        ),
    )(
        trans.reshape(13, 2, 8, 128).transpose(0, 2, 1, 3).reshape(13, 8, 2, 1, 128),
        storage.reshape(2, 8, 128).transpose(1, 0, 2).reshape(8, 2, 1, 128),
        fault_cells.reshape(4, 1, 128),
        fault_trans.reshape(4, 1, 128),
        jnp.broadcast_to(fault_count.reshape(1, 1), (1, 128)),
    )
    return pl.pallas_call(
        body,
        out_shape=jax.ShapeDtypeStruct((125, 1, 256), F32),
        in_specs=[any_space] * 4,
        out_specs=pl.BlockSpec(memory_space=pltpu.VMEM),
        scratch_shapes=[
            pltpu.VMEM((3, 5, 1, 128), jnp.int32),
            pltpu.VMEM((14, 7, 16, 128), F32),
            pltpu.VMEM((3, 5, 4, 1, 128), jnp.int32),
            pltpu.VMEM((3, 5, 4, 1, 128), F32),
            pltpu.SemaphoreType.DMA((4,)),
            pltpu.VMEM((27, 6, 16, 128), F32),
            pltpu.VMEM((6, 16, 128), F32),
            pltpu.VMEM((6, 16, 128), F32),
            pltpu.VMEM((17, 8, 128), F32),
            pltpu.VMEM((3, 12, 24, 128), F32),
            pltpu.VMEM((3, 12, 8, 128), F32),
            pltpu.VMEM((6, 4, 3, 16, 128), F32),
            pltpu.VMEM((3, 6, 12, 4, 8, 128), F32),
            pltpu.VMEM((4, 10, 9, 8, 128), F32),
            pltpu.VMEM((4, 5, 5, 8, 128), F32),
            pltpu.VMEM((5, 5, 4, 8, 64), F32),
        ],
        compiler_params=pltpu.CompilerParams(vmem_limit_bytes=67043328),
    )(slot_n, wide.reshape(14, 7, 16, 128), slot_c, slot_t)


def solution(mesh):
    placed = (
        P(None, "gx", "gy"),
        P("gx", "gy"),
        P("gx", "gy", None),
        P("gx", "gy"),
        P("gx", "gy", None),
    )
    return jax.shard_map(
        per_device, mesh=mesh, in_specs=placed, out_specs=P(None, "gx", "gy"), check_vma=False
    )
```

```python
import jax
import jax.numpy as jnp
from jax import lax
from jax.experimental import pallas as pl
from jax.experimental.pallas import tpu as pltpu
from jax.sharding import PartitionSpec as P

FORWARD = (
    (0, 0, 1),
    (0, 1, -1),
    (0, 1, 0),
    (0, 1, 1),
    (1, -1, -1),
    (1, -1, 0),
    (1, -1, 1),
    (1, 0, -1),
    (1, 0, 0),
    (1, 0, 1),
    (1, 1, -1),
    (1, 1, 0),
    (1, 1, 1),
)
damping = 2.0 / 3.0
tent = 0.35355339059327373
F32 = jnp.float32


def kid(dx, dy, dz):
    return (dx + 1) * 9 + (dy + 1) * 3 + dz + 1


def body(n_any, c_any, fc_any, ft_any, out_ref, counts, c_ref, fc_ref, ft_ref, sems, kf, inv_ref, fd, pat, bands, fp, gs, s3, b3, acc_ref, cols):
    loads = []
    for n, (a, b) in enumerate(
        ((n_any, counts), (fc_any, fc_ref), (ft_any, ft_ref), (c_any, c_ref))
    ):
        loads.append(pltpu.make_async_copy(a, b, sems.at[n]))
        loads[n].start()
    gx = lax.axis_index("gx")
    gy = lax.axis_index("gy")
    odd_dev = lax.rem(gx, 2)
    zl = lax.broadcasted_iota(jnp.int32, (16, 128), 1)
    yi = lax.broadcasted_iota(jnp.int32, (16, 128), 0)
    yg = gy * 8 + yi - 3
    y_in = (yg >= 0) & (yg < 32)
    y_odd = lax.rem(yi, 2) == 0

    e8 = lax.broadcasted_iota(jnp.int32, (8, 128), 0)
    z8 = lax.broadcasted_iota(jnp.int32, (8, 128), 1)
    for d in range(17):
        col = lax.rem(lax.shift_right_logical(z8 + (d - 8 + 160), 1), 5)
        pat[d] = jnp.where(col == e8, F32(1.0), F32(0.0))

    for load in loads:
        load.wait()

    wsum = [jnp.zeros((16, 128), F32) for _ in range(6)]
    for o, (dx, dy, dz) in enumerate(FORWARD):
        ok = y_in & (yg + dy >= 0) & (yg + dy < 32) & (zl + dz >= 0) & (zl + dz < 128)
        for x in range(-3, 4):
            if dx == 0 and x == -3:
                continue
            xg = jnp.full((16, 128), 2 * gx + x, jnp.int32)
            x_ok = (xg >= 0) & (xg + dx < 256)
            m = jnp.where(ok & x_ok, c_ref[o, x + 3], F32(0.0))
            if x >= -2:
                kf[kid(dx, dy, dz), x + 2] = -m
                wsum[x + 2] = wsum[x + 2] + m
            xb = x + dx
            if -2 <= xb <= 3:
                b = m
                if dy:
                    b = pltpu.roll(b, dy % 16, 0)
                if dz:
                    b = pltpu.roll(b, dz % 128, 1)
                kf[kid(-dx, -dy, -dz), xb + 2] = -b
                wsum[xb + 2] = wsum[xb + 2] + b

    x_own = 1 - odd_dev
    x_par = 2 - 3 * odd_dev
    x_oth = 5 * odd_dev - 2
    s_par = 3 - 2 * odd_dev
    s_oth = 1 + 2 * odd_dev
    s_far = 4 * odd_dev
    sides = ((2, s_par, 2), (s_par, 2, 2), (s_oth, s_far, s_oth))

    def slot_row(ref, dev, place):
        return jnp.concatenate([ref[dev, place, i] for i in range(4)], axis=1)

    zrow = lax.broadcasted_iota(jnp.int32, (128, 512), 0)
    slot = lax.broadcasted_iota(jnp.int32, (1, 512), 1)
    for dev, (ylo, ny, yout) in enumerate(((6, 2, 0), (0, 8, 2), (0, 2, 10))):
        for side, (own, par, tr) in enumerate(sides):
            co = slot_row(fc_ref, dev, own) & 1023
            cp = slot_row(fc_ref, dev, par) & 1023
            reach = (gy + dev >= 1) & (gy + dev < 5)
            if side == 2:
                mate = gx + 4 * odd_dev - 2
                reach = reach & (mate >= 0) & (mate < 128)
            count = jnp.concatenate([counts[dev, tr]] * 4, axis=1)
            alive = jnp.where(jnp.full((1, 512), reach.astype(jnp.int32)) > 0, count, 0)
            t = jnp.where(slot < alive, slot_row(ft_ref, dev, tr), F32(0.0))
            zo = co & 127
            key = (lax.shift_right_logical(co, 7) - ylo) * 24 + (cp & 127) - zo + 8
            hit = lax.broadcasted_iota(jnp.int32, (ny * 24, 512), 0) == key
            hi = t.astype(jnp.bfloat16).astype(F32)
            mid = (t - hi).astype(jnp.bfloat16).astype(F32)
            parts = [
                jnp.where(hit, p, F32(0.0)).astype(jnp.bfloat16) for p in (hi, mid, t - hi - mid)
            ]
            hot = jnp.where(zrow == zo, F32(1.0), F32(0.0)).astype(jnp.bfloat16)
            got = lax.dot_general(
                jnp.concatenate(parts, axis=0),
                hot,
                (((1,), (1,)), ((), ())),
                preferred_element_type=F32,
            )
            n = ny * 24
            got = got[:n] + got[n : 2 * n] + got[2 * n :]
            bands[side, yout : yout + ny] = got.reshape(ny, 24, 128)

    fd[...] = jnp.zeros((6, 16, 128), F32)

    def probe_fault(y, carry):
        for side, xs in enumerate((x_own, x_par, x_oth)):
            tile = jnp.zeros((8, 128), F32)
            for d in range(17):
                tile = tile + bands[side, y, d : d + 1, :] * pat[d]
            fp[side, y] = tile
            fd[xs + 2, pl.ds(y + 1, 1), :] = jnp.sum(tile, axis=0, keepdims=True)
        return carry

    lax.fori_loop(0, 12, probe_fault, 0)

    for x in range(-2, 4):
        diag = c_ref[13, x + 3] + wsum[x + 2] + fd[x + 2]
        xg = jnp.full((16, 128), 2 * gx + x, jnp.int32)
        inv = jnp.where(y_in & (xg >= 0) & (xg < 256), 1.0 / diag, F32(0.0))
        diag = jnp.where(y_in & (xg >= 0) & (xg < 256), diag, F32(0.0))
        kf[13, x + 2] = diag
        inv_ref[x + 2] = inv
        for dz in (-1, 0, 1):
            low, high = [], []
            for dx in (-1, 0, 1):
                mid = kf[kid(dx, 0, dz), x + 2]
                low.append(kf[kid(dx, -1, dz), x + 2] + jnp.where(y_odd, mid, F32(0.0)))
                high.append(kf[kid(dx, 1, dz), x + 2] + jnp.where(y_odd, F32(0.0), mid))
            for ry, part in enumerate((low, high)):
                if x % 2:
                    pair = (part[0] + part[1], part[2])
                else:
                    pair = (part[0], part[1] + part[2])
                for rx, total in enumerate(pair):
                    g = inv * total * F32(-damping * tent)
                    if dz == 0 and rx == (0 if x % 2 else 1):
                        mine = y_odd if ry == 0 else jnp.logical_not(y_odd)
                        g = g + jnp.where(mine, F32(tent), F32(0.0))
                    gs[x + 2, rx * 2 + ry, dz + 1] = g

    def smooth(y, carry):
        for x in range(6):
            for r in range(4):
                tile = gs[x, r, 0, pl.ds(y + 1, 1), :] * pat[7]
                tile = tile + gs[x, r, 1, pl.ds(y + 1, 1), :] * pat[8]
                tile = tile + gs[x, r, 2, pl.ds(y + 1, 1), :] * pat[9]
                s3[1, x, y, r] = tile
                s3[0, x, y, r] = pltpu.roll(tile, 1, 1)
                s3[2, x, y, r] = pltpu.roll(tile, 127, 1)
        ry = 1 - lax.rem(y, 2)
        for side, xs in enumerate((x_own, x_par, x_oth)):
            rx = xs & 1
            iv = inv_ref[xs + 2, pl.ds(y + 1, 1), :] * F32(damping * tent)
            tile = s3[1, xs + 2, y, rx * 2 + ry] + iv * fp[side, y]
            s3[1, xs + 2, y, rx * 2 + ry] = tile
            s3[0, xs + 2, y, rx * 2 + ry] = pltpu.roll(tile, 1, 1)
            s3[2, xs + 2, y, rx * 2 + ry] = pltpu.roll(tile, 127, 1)
        return carry

    lax.fori_loop(0, 12, smooth, 0)

    def apply_pair(t, carry):
        for x in range(-1, 3):
            for p in range(2):
                y = p - 1
                acc = [None] * 9
                for dx in (-1, 0, 1):
                    for dy in (-1, 0, 1):
                        xn, yn = x + dx, y + dy
                        bx = (xn - 1) // 2 - (x // 2 - 1)
                        by = (yn - 1) // 2 - (y // 2 - 1)
                        for dz in (-1, 0, 1):
                            row = kf[kid(dx, dy, dz), x + 2, pl.ds(2 * t + y + 3, 1), :]
                            for rx in range(2):
                                for ry in range(2):
                                    q = (bx + rx) * 3 + by + ry
                                    v = row * s3[dz + 1, xn + 2, 2 * t + yn + 2, rx * 2 + ry]
                                    acc[q] = v if acc[q] is None else acc[q] + v
                iv = inv_ref[x + 2, pl.ds(2 * t + y + 3, 1), :]
                for q in range(9):
                    tile = acc[q] * iv
                    b3[x + 1, 2 * t + y + 1, q] = tile
        return carry

    lax.fori_loop(0, 5, apply_pair, 0)

    def apply_fault(n, carry):
        y_is_odd = (n - 1) & 1
        for side, (xs, xn) in enumerate(((x_own, x_par), (x_par, x_own))):
            iv = inv_ref[xs + 2, pl.ds(n + 2, 1), :]
            done = []
            for r in range(4):
                tile = s3[1, xn + 2, n + 1, r]
                total = jnp.zeros((8, 128), F32)
                for d in range(17):
                    row = bands[side, n + 1, d : d + 1, :]
                    total = total + row * pltpu.roll(tile, (8 - d) % 128, 1)
                q = ((xs & 1) + r // 2) * 3 + y_is_odd + r % 2
                done.append((q, b3[xs + 1, n, q] - total * iv))
            for q, tile in done:
                b3[xs + 1, n, q] = tile
        return carry

    lax.fori_loop(0, 10, apply_fault, 0)

    pz = lax.broadcasted_iota(jnp.int32, (128, 64), 0)
    pc = lax.broadcasted_iota(jnp.int32, (128, 64), 1)
    pick = jnp.where(lax.shift_right_logical(pz, 1) == pc, F32(tent), F32(0.0))

    def restrict(yc, carry):
        for dz in (-1, 1, 0):
            acc = [None] * 25
            for xn in range(-1, 3):
                for yn in range(-1, 3):
                    bx, by = xn // 2 + 1, yn // 2 + 1
                    row = None
                    for x in (0, 1):
                        for y in (0, 1):
                            if abs(xn - x) <= 1 and abs(yn - y) <= 1:
                                k = kf[kid(xn - x, yn - y, dz), x + 2, pl.ds(2 * yc + y + 3, 1), :]
                                row = k if row is None else row + k
                    row = row * F32(-damping)
                    if dz == 0 and xn in (0, 1) and yn in (0, 1):
                        row = row + kf[13, xn + 2, pl.ds(2 * yc + yn + 3, 1), :]
                    row = jnp.broadcast_to(row, (8, 128))
                    if dz:
                        row = pltpu.roll(row, dz % 128, 1)
                    for rx in range(3):
                        for ry in range(3):
                            q = (bx + rx) * 5 + by + ry
                            v = row * b3[xn + 1, 2 * yc + yn + 1, rx * 3 + ry]
                            acc[q] = v if acc[q] is None else acc[q] + v
            for q in range(25):
                v = pltpu.roll(acc[q], -dz % 128, 1) if dz else acc[q]
                acc_ref[yc, q // 5, q % 5] = v if dz == -1 else acc_ref[yc, q // 5, q % 5] + v
        far = lax.shift_right_arithmetic(x_par, 1) + 1
        for rx in range(3):
            for ry in range(3):
                total = jnp.zeros((8, 128), F32)
                for y in range(2):
                    tile = b3[x_par + 1, 2 * yc + y + 1, rx * 3 + ry]
                    for d in range(17):
                        row = bands[0, 2 * yc + y + 2, d : d + 1, :]
                        total = total + row * pltpu.roll(tile, (8 - d) % 128, 1)
                acc_ref[yc, far + rx, 1 + ry] += total * F32(damping)
        return carry

    lax.fori_loop(0, 4, restrict, 0)
    got = jnp.dot(
        acc_ref[...].reshape(800, 128),
        pick,
        precision=lax.Precision.HIGHEST,
        preferred_element_type=F32,
    )
    for yc in range(4):
        for rx in range(5):
            a = lax.rem(gx + rx + 3, 5)
            for ry in range(5):
                b = lax.rem(gy * 4 + yc + ry + 3, 5)
                q = (yc * 25 + rx * 5 + ry) * 8
                cols[a, b, yc] = got[q : q + 8]
    for a in range(5):
        for b in range(5):
            tile = jnp.concatenate([cols[a, b, yc] for yc in range(4)], axis=1)
            c = (a * 5 + b) * 5
            out_ref[c : c + 5, 0, :] = tile[:5]


SOURCES = (
    (-2, 0, 1, 1, 4, 9),
    (-1, 1, 2, 0, 0, 14),
    (0, 3, 2, 0, 0, 14),
    (1, 5, 2, 0, 0, 14),
    (2, None, 0, 0, 0, 0),
)


def exchange(trans, storage, cells, weights, count, wide, slot_c, slot_t, slot_n, send, recv, ysend, yrecv, local):
    gx = lax.axis_index("gx")
    gy = lax.axis_index("gy")

    def has(i):
        return (gx + i >= 0) & (gx + i < 128)

    def has_y(j):
        return (gy + j >= 0) & (gy + j < 4)

    barrier = pltpu.get_barrier_semaphore()
    count_in = 0
    for i in (-2, -1, 1, 2):
        count_in = count_in + has(i).astype(jnp.int32)

        @pl.when(has(i))
        def _(i=i):
            pl.semaphore_signal(
                barrier, inc=1, device_id=(gx + i, gy), device_id_type=pl.DeviceIdType.MESH
            )

    for j in (-1, 1):
        count_in = count_in + has_y(j).astype(jnp.int32)

        @pl.when(has_y(j))
        def _(j=j):
            pl.semaphore_signal(
                barrier, inc=1, device_id=(gx, gy + j), device_id_type=pl.DeviceIdType.MESH
            )

    def faults(n):
        return ((cells, slot_c, n), (weights, slot_t, n), (count, slot_n, n))

    keeps = []
    for x in range(2):
        keeps.append((trans.at[:, :, x], wide.at[0:13, 3 + x, 3:11]))
        keeps.append((storage.at[:, x], wide.at[13, 3 + x, 3:11]))
    for own, slots, n in faults(2):
        keeps.append((own, slots.at[1, n]))
    keeps = [pltpu.make_async_copy(a, b, local.at[n]) for n, (a, b) in enumerate(keeps)]
    for k in keeps:
        k.start()
    pl.semaphore_wait(barrier, count_in)

    def remote(pairs, sends, recvs, to):
        return [
            pltpu.make_async_remote_copy(
                a,
                b,
                sends.at[k],
                recvs.at[k],
                device_id=to,
                device_id_type=pl.DeviceIdType.MESH,
            )
            for k, (a, b) in enumerate(pairs)
        ]

    def along_x(n):
        i, x0, nx, own, o0, no = SOURCES[n]
        pairs = []
        for x in range(nx):
            last = min(o0 + no, 13)
            pairs.append((trans.at[o0:last, :, own + x], wide.at[o0:last, x0 + x, 3:11]))
            if no == 14:
                pairs.append((storage.at[:, own + x], wide.at[13, x0 + x, 3:11]))
        pairs += [(a, slots.at[1, m]) for a, slots, m in faults(n)]
        return remote(pairs, send.at[n], recv.at[n], (gx - i, gy))

    def along_y(n, j):
        i, x0, nx, own, o0, no = SOURCES[n]
        y0, y1 = (8, 0) if j == 1 else (3, 11)
        place = 0 if j == 1 else 2
        pairs = []
        if n == 2:
            for x in range(2):
                pairs.append(
                    (trans.at[:, y0 - 3 : y0, x], wide.at[0:13, 3 + x, y1 : y1 + 3])
                )
                pairs.append((storage.at[y0 - 3 : y0, x], wide.at[13, 3 + x, y1 : y1 + 3]))
        elif no:
            cut = wide.at[o0 : o0 + no, x0 : x0 + nx]
            pairs.append((cut.at[:, :, y0 : y0 + 3], cut.at[:, :, y1 : y1 + 3]))
        for a, slots, m in faults(n):
            pairs.append((a if n == 2 else slots.at[1, m], slots.at[place, m]))
        s = (j + 1) // 2
        return remote(pairs, ysend.at[s, n], yrecv.at[s, n], (gx, gy + j))

    def guarded(ok, copies, what):
        @pl.when(ok)
        def _():
            for c in copies:
                getattr(c, what)()

    for n in (0, 1, 3, 4):
        guarded(has(-SOURCES[n][0]), along_x(n), "start")
    for j in (-1, 1):
        guarded(has_y(j), along_y(2, j), "start")
    for n in (1, 3, 4, 0):
        guarded(has(SOURCES[n][0]), along_x(n), "wait_recv")
        for j in (-1, 1):
            guarded(has(SOURCES[n][0]) & has_y(j), along_y(n, j), "start")
    for n in (0, 1, 3, 4):
        guarded(has(-SOURCES[n][0]), along_x(n), "wait_send")
    for n in range(5):
        for j in (-1, 1):
            guarded(has(SOURCES[n][0]) & has_y(j), along_y(n, j), "wait_send")
            guarded(has(SOURCES[n][0]) & has_y(-j), along_y(n, j), "wait_recv")
    for k in keeps:
        k.wait()


def per_device(trans, storage, fault_cells, fault_count, fault_trans):
    any_space = pl.BlockSpec(memory_space=pltpu.HBM)
    wide, slot_c, slot_t, slot_n = pl.pallas_call(
        exchange,
        out_shape=(
            jax.ShapeDtypeStruct((14, 7, 16, 1, 128), F32),
            jax.ShapeDtypeStruct((3, 5, 4, 1, 128), jnp.int32),
            jax.ShapeDtypeStruct((3, 5, 4, 1, 128), F32),
            jax.ShapeDtypeStruct((3, 5, 1, 128), jnp.int32),
        ),
        in_specs=[any_space] * 5,
        out_specs=(any_space,) * 4,
        scratch_shapes=[
            pltpu.SemaphoreType.DMA((5, 7)),
            pltpu.SemaphoreType.DMA((5, 7)),
            pltpu.SemaphoreType.DMA((2, 5, 7)),
            pltpu.SemaphoreType.DMA((2, 5, 7)),
            pltpu.SemaphoreType.DMA((7,)),
        ],
        compiler_params=pltpu.CompilerParams(
            collective_id=0, has_side_effects=True, vmem_limit_bytes=67043328
        ),
    )(
        trans.reshape(13, 2, 8, 128).transpose(0, 2, 1, 3).reshape(13, 8, 2, 1, 128),
        storage.reshape(2, 8, 128).transpose(1, 0, 2).reshape(8, 2, 1, 128),
        fault_cells.reshape(4, 1, 128),
        fault_trans.reshape(4, 1, 128),
        jnp.broadcast_to(fault_count.reshape(1, 1), (1, 128)),
    )
    return pl.pallas_call(
        body,
        out_shape=jax.ShapeDtypeStruct((125, 1, 256), F32),
        in_specs=[any_space] * 4,
        out_specs=pl.BlockSpec(memory_space=pltpu.VMEM),
        scratch_shapes=[
            pltpu.VMEM((3, 5, 1, 128), jnp.int32),
            pltpu.VMEM((14, 7, 16, 128), F32),
            pltpu.VMEM((3, 5, 4, 1, 128), jnp.int32),
            pltpu.VMEM((3, 5, 4, 1, 128), F32),
            pltpu.SemaphoreType.DMA((4,)),
            pltpu.VMEM((27, 6, 16, 128), F32),
            pltpu.VMEM((6, 16, 128), F32),
            pltpu.VMEM((6, 16, 128), F32),
            pltpu.VMEM((17, 8, 128), F32),
            pltpu.VMEM((3, 12, 24, 128), F32),
            pltpu.VMEM((3, 12, 8, 128), F32),
            pltpu.VMEM((6, 4, 3, 16, 128), F32),
            pltpu.VMEM((3, 6, 12, 4, 8, 128), F32),
            pltpu.VMEM((4, 10, 9, 8, 128), F32),
            pltpu.VMEM((4, 5, 5, 8, 128), F32),
            pltpu.VMEM((5, 5, 4, 8, 64), F32),
        ],
        compiler_params=pltpu.CompilerParams(vmem_limit_bytes=67043328),
    )(slot_n, wide.reshape(14, 7, 16, 128), slot_c, slot_t)


def solution(mesh):
    placed = (
        P(None, "gx", "gy"),
        P("gx", "gy"),
        P("gx", "gy", None),
        P("gx", "gy"),
        P("gx", "gy", None),
    )
    return jax.shard_map(
        per_device, mesh=mesh, in_specs=placed, out_specs=P(None, "gx", "gy"), check_vma=False
    )
```
